32 devices in a mesh: seq: 8 (over y, x, core), red: 4 (over z).
Axes of the slice: x: 2, y: 2, z: 4, core: 2. Of those that a mesh axis runs over, the one named last changes fastest.
Arguments:
- token_ids: int32 [1024], P('seq'), may hold values from 0 to 511
- embedding: bfloat16 [512, 4096], P(None, 'red'), may hold values from -6 to 6
- proj_weight: bfloat16 [4096, 3, 4, 256], P('red', None, None, 'seq'), may hold values from -0.09375 to 0.09375
- filters: float32 [1024, 1024], P('seq', 'red'), may hold values from -1 to 1
- cotangent: float32 [1024, 1024], P('seq', 'red'), may hold values from -6 to 6
Outputs:
- output: float32 [1024, 1024], P('seq', 'red')
- filter_grad: float32 [1024, 1024], P('seq', 'red')
- branch_grads: bfloat16 [1024, 3, 1024], P('seq', None, 'red')
- weight_grad: float32 [4096, 3, 4, 256], P('red', None, None, 'seq')
The draws below stay inside these ranges and needn't reach their ends.
All inputs are finite; a program needn't handle non-finite values.
Results may differ from the reference program's by a relative error of at most 0.0029.
Values sent between devices are 32-bit elements; how exact they have to be, the bound alone decides.
A program may use at most 64 MiB of HBM per device.

```python
import math
import jax
import jax.numpy as jnp
from jax import lax

D = 4096
C = 1024
VOCAB = 512
TOKENS = 1024
N_RED = 4


def draw_filters(key, part):
    rate_key, pick_key, noise_key, fast_key = jax.random.split(key, 4)
    positions = jnp.arange(TOKENS, dtype=jnp.float32)[:, None]
    slow_rates = jnp.exp(jax.random.uniform(rate_key, (C,), jnp.float32, math.log(0.1 / TOKENS), math.log(2.3 / TOKENS)))
    fast_rates = jnp.exp(jax.random.uniform(fast_key, (C,), jnp.float32, math.log(2.3 / TOKENS), math.log(1.0 / 30.0)))
    picked = jax.random.uniform(pick_key, (C,), jnp.float32)
    keeping = picked < 0.5
    noise = jnp.clip(jax.random.normal(noise_key, (TOKENS, C), jnp.float32), -4.0, 4.0)
    rates = jnp.where(keeping, slow_rates, fast_rates)
    shaped = noise * jnp.exp(-positions * rates[None, :])
    return shaped * jax.lax.rsqrt(jnp.sum(shaped * shaped, axis=0, keepdims=True))


def touch_ends(array, stream_key, least, largest):
    index_at = [jax.random.randint(jax.random.fold_in(stream_key, axis), (), 0, length) for axis, length in enumerate(array.shape)]
    main_axis = array.shape.index(max(array.shape))
    beside = index_at[:main_axis] + [(index_at[main_axis] + 1) % array.shape[main_axis]] + index_at[main_axis + 1:]
    return array.at[tuple(index_at)].set(least).at[tuple(beside)].set(largest)


def steps_of(rng, shape, shards, low, largest):
    level, own = 1.0, jax.random.fold_in(rng, 6)
    for axis_at, blocks in shards:
        steps = jnp.exp(jax.random.uniform(jax.random.fold_in(own, axis_at), (blocks,), jnp.float32, low / len(shards), largest / len(shards)))
        level = level * jnp.repeat(steps, shape[axis_at] // blocks).reshape([-1 if axis == axis_at else 1 for axis in range(len(shape))])
    return level


def scatter_about(rng, dims, width, most, shards=(), kind=jnp.bfloat16):
    array = jax.random.normal(rng, dims, jnp.float32) * width
    if len(shards) > 0:
        array = steps_of(rng, dims, shards, -0.22, 0.18) * array
    return jnp.clip(array, min=-most, max=most).astype(kind)


def setup_inputs(seed: int = 0) -> dict:
    arg_keys = jax.random.split(jax.random.key(seed), 6)
    return {
        "token_ids": touch_ends(jax.random.randint(arg_keys[0], (TOKENS,), 0, VOCAB), jax.random.fold_in(arg_keys[0], 1), 0, VOCAB - 1).astype(jnp.int32),
        "embedding": scatter_about(arg_keys[1], (VOCAB, D), 1.0, 6.0, ((1, 4),)),
        "proj_weight": scatter_about(arg_keys[2], (D, 3, N_RED, C // N_RED), D ** -0.5, 0.09375, ((0, 4), (3, 8))),
        "filters": draw_filters(jax.random.fold_in(arg_keys[5], 71), 0),
        "cotangent": scatter_about(arg_keys[4], (TOKENS, C), 1.0, 6.0, ((0, 8), (1, 4)), jnp.float32),
    }


def reference(token_ids, embedding, proj_weight, filters, cotangent):
    weight_matrix = proj_weight.reshape(D, 3 * C)
    lookup = jnp.dot(embedding, weight_matrix, preferred_element_type=jnp.float32)
    projected = jnp.take(lookup, token_ids, axis=0)
    queries = projected[:, :C]
    key_rows = projected[:, C:2 * C]
    value_rows = projected[:, 2 * C:]
    inner = key_rows * value_rows
    upstream = cotangent * queries
    length = token_ids.shape[0]
    padded = 2 * length
    spectra = jnp.fft.rfft(jnp.concatenate([filters, inner, upstream], axis=1), n=padded, axis=0)
    filt_spec = spectra[:, :C]
    inner_spec = spectra[:, C:2 * C]
    up_spec = spectra[:, 2 * C:]
    joined = jnp.concatenate([filt_spec * inner_spec, jnp.conj(filt_spec) * up_spec, up_spec * jnp.conj(inner_spec)], axis=1)
    back = jnp.fft.irfft(joined, n=padded, axis=0)[:length]
    conv = back[:, :C]
    grad_inner = back[:, C:2 * C]
    filter_raw = back[:, 2 * C:]
    scale_factor = float(TOKENS) ** -0.5
    output = queries * conv
    filter_grad = filter_raw * scale_factor
    branch_grads = jnp.stack([cotangent * conv, grad_inner * value_rows, grad_inner * key_rows], axis=1).astype(jnp.bfloat16)
    summed = jax.ops.segment_sum(branch_grads.reshape(length, 3 * C).astype(jnp.float32), token_ids, num_segments=VOCAB)
    weight_grad = jnp.dot(embedding.astype(jnp.float32).T, summed, precision=lax.Precision.HIGHEST) * scale_factor
    return output, filter_grad, branch_grads, weight_grad.reshape(D, 3, N_RED, C // N_RED)
```

```python
import functools
import math

import jax
import jax.numpy as jnp
import numpy as np
from jax import lax
from jax.experimental import pallas as pl
from jax.experimental.pallas import tpu as pltpu
from jax.sharding import PartitionSpec as P

precise_mode = lax.Precision.HIGHEST
MESH = pl.DeviceIdType.MESH
VMEM = pl.BlockSpec(memory_space=pltpu.VMEM)
NN = (((1,), (0,)), ((), ()))
NT = (((1,), (1,)), ((), ()))


def split(value):
    high = value.astype(jnp.bfloat16)
    low = (value - high.astype(jnp.float32)).astype(jnp.bfloat16)
    return high, low


def dot(left, right, dims=NN):
    return lax.dot_general(left, right, dims, preferred_element_type=jnp.float32)


def dot_split(value, matrix, dims=NN):
    high, low = split(value)
    both = dot(jnp.concatenate([high, low], axis=0), matrix, dims)
    rows = value.shape[0]
    return both[:rows] + both[rows:]


def dot_both(value, matrix_high, matrix_low, dims=NN):
    high, _ = split(value)
    return dot_split(value, matrix_high, dims) + dot(high, matrix_low, dims)


def transform_tables(block, blocks):
    total = 2 * blocks * block
    place = np.arange(block)
    half = block // 2
    tables = np.zeros((blocks, 2 * block, 2 * block))
    even = 2 * np.pi * ((2 * blocks * place[:, None] * np.arange(half)[None, :]) % total) / total
    odd = 2 * np.pi * ((place[:, None] * (blocks + 2 * blocks * np.arange(half))[None, :]) % total) / total
    tables[0, :block, :half] = np.cos(even)
    tables[0, :block, block : block + half] = np.sin(even)
    tables[0, :block, block] = 1.0 - 2.0 * (place % 2)
    tables[0, block:, half:block] = np.cos(odd)
    tables[0, block:, block + half :] = np.sin(odd)
    for residue in range(1, blocks):
        freq = residue + 2 * blocks * np.arange(block)
        psi = 2 * np.pi * ((place[:, None] * freq[None, :]) % total) / total
        tables[residue, :block, :block] = np.cos(psi)
        tables[residue, :block, block:] = np.sin(psi)
        tables[residue, block:, :block] = -np.sin(psi)
        tables[residue, block:, block:] = np.cos(psi)
    tables = tables.astype(np.float32)
    high = tables.astype(jnp.bfloat16)
    low = (tables - high.astype(np.float32)).astype(jnp.bfloat16)
    return high, low


def phases(residue, blocks):
    if residue == 0:
        return [1.0] * blocks, [(-1.0) ** index for index in range(blocks)]
    turn = [math.pi * ((residue * index) % (2 * blocks)) / blocks for index in range(blocks)]
    return [math.cos(a) for a in turn], [math.sin(a) for a in turn]


def weighted(terms, weights):
    total = None
    for term, weight in zip(terms, weights):
        if abs(weight) < 1e-12:
            continue
        part = term if weight == 1.0 else term * weight
        total = part if total is None else total + part
    return total


def greet(devices, count):
    me = lax.axis_index("seq")
    spot = lax.axis_index("red")
    barrier = pltpu.get_barrier_semaphore()
    for step in range(1, devices):
        peer = lax.rem(me + step, devices)
        pl.semaphore_signal(barrier, inc=1, device_id={"seq": peer}, device_id_type=MESH)

    @pl.when(spot > 0)
    def _():
        pl.semaphore_signal(barrier, inc=1, device_id={"red": spot - 1}, device_id_type=MESH)

    @pl.when(spot < count - 1)
    def _():
        pl.semaphore_signal(barrier, inc=1, device_id={"red": spot + 1}, device_id_type=MESH)

    neighbours = jnp.where(spot > 0, 1, 0) + jnp.where(spot < count - 1, 1, 0)
    pl.semaphore_wait(barrier, devices - 1 + neighbours)


def exchange(devices, source, target, send_sem, recv_sem):
    me = lax.axis_index("seq")
    copies = []
    for step in range(1, devices):
        peer = lax.rem(me + step, devices)
        copy = pltpu.make_async_remote_copy(
            src_ref=source.at[peer],
            dst_ref=target.at[me],
            send_sem=send_sem.at[step - 1],
            recv_sem=recv_sem.at[step - 1],
            device_id={"seq": peer},
            device_id_type=MESH,
        )
        copy.start()
        copies.append(copy)
    return copies


def gather_kernel(
    devices, count, tok_ref, emb_ref, wt_ref, filt_ref, cot_ref,
    own_ref, sig_ref,
    part, from_left, from_right, out_sig,
    send_sig, recv_sig, send_right, recv_right, send_left, recv_left,
):
    me = lax.axis_index("seq")
    spot = lax.axis_index("red")
    branches, _, piece, _ = wt_ref.shape
    tok_count, width = filt_ref.shape
    filt_t = filt_ref[...].T
    cot_t = cot_ref[...].T
    tok_rows = jnp.broadcast_to(tok_ref[...].astype(jnp.float32), (8, tok_count))
    for peer in range(devices):
        out_sig[peer, :piece] = filt_t[peer * piece : (peer + 1) * piece]
        out_sig[peer, piece : 2 * piece] = cot_t[peer * piece : (peer + 1) * piece]
        out_sig[peer, 2 * piece :] = tok_rows
    greet(devices, count)
    copies = exchange(devices, out_sig, sig_ref, send_sig, recv_sig)
    table = emb_ref[...]
    for group in range(count):
        rows = jnp.concatenate([wt_ref[branch, group] for branch in range(branches)], axis=0)
        part[group] = dot(rows, table, NT)
    sig_ref[me] = out_sig[me]

    def hop(slot, target, sends, recvs, neighbour):
        return pltpu.make_async_remote_copy(
            src_ref=part.at[slot],
            dst_ref=target.at[slot],
            send_sem=sends.at[slot],
            recv_sem=recvs.at[slot],
            device_id={"red": neighbour},
            device_id_type=MESH,
        )

    right = functools.partial(
        hop, target=from_left, sends=send_right, recvs=recv_right,
        neighbour=jnp.minimum(spot + 1, count - 1),
    )
    left = functools.partial(
        hop, target=from_right, sends=send_left, recvs=recv_left,
        neighbour=jnp.maximum(spot - 1, 0),
    )
    for step in range(count - 1):
        goal = count - 1 - step

        @pl.when(spot < goal)
        def _():
            @pl.when(spot > 0)
            def _():
                right(goal).wait_recv()
                part[goal] = part[goal] + from_left[goal]

            right(goal).start()

        other = step

        @pl.when(spot > other)
        def _():
            @pl.when(spot < count - 1)
            def _():
                left(other).wait_recv()
                part[other] = part[other] + from_right[other]

            left(other).start()

    for goal in range(count):
        @pl.when(spot == goal)
        def _():
            total = part[goal]
            if goal > 0:
                right(goal).wait_recv()
                total = total + from_left[goal]
            if goal < count - 1:
                left(goal).wait_recv()
                total = total + from_right[goal]
            own_ref[...] = total

        @pl.when(spot < goal)
        def _():
            right(goal).wait_send()

        @pl.when(spot > goal)
        def _():
            left(goal).wait_send()

    for copy in copies:
        copy.wait()


def convolve(signals, high_ref, low_ref, piece):
    blocks, double, _ = high_ref.shape
    block = double // 2
    pieces = [signals[:, index * block : (index + 1) * block] for index in range(blocks)]
    results = [None] * blocks
    scale = 1.0 / (blocks * block)
    for residue in range(blocks):
        cosines, sines = phases(residue, blocks)
        packed = jnp.concatenate([weighted(pieces, cosines), weighted(pieces, sines)], axis=1)
        spectrum = dot_both(packed, high_ref[residue], low_ref[residue])
        cos_part = spectrum[:, :block]
        sin_part = spectrum[:, block:]
        fc, ic, uc = (cos_part[at * piece : (at + 1) * piece] for at in range(3))
        fs, i_s, us = (sin_part[at * piece : (at + 1) * piece] for at in range(3))
        cc = [fc * ic, fc * uc, uc * ic]
        ss = [fs * i_s, fs * us, us * i_s]
        signs = [-1.0, 1.0, 1.0]
        new_cos = [c + sign * s for c, s, sign in zip(cc, ss, signs)]
        new_sin = [fc * i_s + fs * ic, fc * us - fs * uc, us * ic - uc * i_s]
        new_cos = jnp.concatenate(new_cos, axis=0)
        new_sin = jnp.concatenate(new_sin, axis=0)
        if residue == 0:
            first = lax.broadcasted_iota(jnp.int32, new_cos.shape, 1) == 0
            new_cos = jnp.where(first, 0.5 * jnp.concatenate(cc, axis=0), new_cos)
            new_sin = jnp.where(first, 0.5 * jnp.concatenate(ss, axis=0), new_sin)
        joined = jnp.concatenate([new_cos, new_sin], axis=1) * scale
        back = dot_both(joined, high_ref[residue], low_ref[residue], NT)
        first_half = back[:, :block]
        second_half = back[:, block:]
        for index in range(blocks):
            term = weighted([first_half, second_half], [cosines[index], sines[index]])
            results[index] = term if results[index] is None else results[index] + term
    return results


def middle_kernel(scale_factor, own_ref, sig_ref, high_ref, low_ref, send_ref, sums_ref):
    vocabulary = own_ref.shape[1]
    devices, _, block = sig_ref.shape
    piece = own_ref.shape[0] // 3
    ids = jnp.concatenate([sig_ref[at, 2 * piece : 2 * piece + 1] for at in range(devices)], axis=1)
    length = devices * block
    rows = lax.broadcasted_iota(jnp.int32, (vocabulary, length), 0)
    one_hot = jnp.where(rows == ids.astype(jnp.int32), 1.0, 0.0).astype(jnp.bfloat16)
    projected = dot_split(own_ref[...], one_hot)
    queries = projected[:piece]
    key_rows = projected[piece : 2 * piece]
    value_rows = projected[2 * piece :]
    filters = jnp.concatenate([sig_ref[at, :piece] for at in range(devices)], axis=1)
    cotangent = jnp.concatenate([sig_ref[at, piece : 2 * piece] for at in range(devices)], axis=1)
    signals = jnp.concatenate([filters, key_rows * value_rows, cotangent * queries], axis=0)
    results = convolve(signals, high_ref, low_ref, piece)
    rounded = []
    for at in range(devices):
        lanes = slice(at * block, (at + 1) * block)
        conv = results[at][:piece]
        grad_inner = results[at][piece : 2 * piece]
        grads = jnp.concatenate(
            [
                cotangent[:, lanes] * conv,
                grad_inner * value_rows[:, lanes],
                grad_inner * key_rows[:, lanes],
            ],
            axis=0,
        ).astype(jnp.bfloat16)
        rounded.append(grads)
        send_ref[at, :piece] = queries[:, lanes] * conv
        send_ref[at, piece : 2 * piece] = results[at][2 * piece :] * scale_factor
        send_ref[at, 2 * piece :] = grads.astype(jnp.float32)
    sums_ref[...] = dot(jnp.concatenate(rounded, axis=1), one_hot, NT)


def return_kernel(
    devices, count, send_ref, sums_ref, recv_ref, all_ref,
    send_sem, recv_sem, send_right, recv_right, send_left, recv_left,
):
    me = lax.axis_index("seq")
    spot = lax.axis_index("red")
    greet(devices, count)

    def hop(source, slot, sends, recvs, neighbour):
        return pltpu.make_async_remote_copy(
            src_ref=source,
            dst_ref=all_ref.at[slot],
            send_sem=sends.at[slot],
            recv_sem=recvs.at[slot],
            device_id={"red": neighbour},
            device_id_type=MESH,
        )

    def right(source, slot):
        return hop(source, slot, send_right, recv_right, jnp.minimum(spot + 1, count - 1))

    def left(source, slot):
        return hop(source, slot, send_left, recv_left, jnp.maximum(spot - 1, 0))

    @pl.when(spot < count - 1)
    def _():
        right(sums_ref, spot).start()

    @pl.when(spot > 0)
    def _():
        left(sums_ref, spot).start()

    copies = exchange(devices, send_ref, recv_ref, send_sem, recv_sem)
    all_ref[spot] = sums_ref[...]
    recv_ref[me] = send_ref[me]
    for step in range(1, count):
        below = spot - step

        @pl.when(below >= 0)
        def _():
            right(all_ref.at[below], below).wait_recv()

            @pl.when(spot < count - 1)
            def _():
                right(all_ref.at[below], below).start()

        above = spot + step

        @pl.when(above < count)
        def _():
            left(all_ref.at[above], above).wait_recv()

            @pl.when(spot > 0)
            def _():
                left(all_ref.at[above], above).start()

    for step in range(count):
        @pl.when((spot - step >= 0) & (spot < count - 1))
        def _():
            right(sums_ref, spot - step).wait_send()

        @pl.when((spot + step < count) & (spot > 0))
        def _():
            left(sums_ref, spot + step).wait_send()

    for copy in copies:
        copy.wait()


def final_kernel(scale_factor, emb_ref, recv_ref, all_ref, out_ref, filt_ref, grads_ref, weight_ref):
    devices, rows, _ = recv_ref.shape
    piece = rows // 5
    count = all_ref.shape[0]
    table = emb_ref[...]
    for group in range(count):
        product = dot_split(all_ref[group], table) * scale_factor
        for branch in range(3):
            weight_ref[branch, group] = product[branch * piece : (branch + 1) * piece]

    def positions(at):
        parts = [recv_ref[peer, at * piece : (at + 1) * piece] for peer in range(devices)]
        return jnp.concatenate(parts, axis=0).T

    out_ref[...] = positions(0)
    filt_ref[...] = positions(1)
    for branch in range(3):
        grads_ref[branch] = positions(2 + branch).astype(jnp.bfloat16)


def kernel_shards(devices, count, token_ids, embedding, proj_weight, filters, cotangent):
    tok_count, width = filters.shape
    vocabulary, depth = embedding.shape
    _, branches, _, piece = proj_weight.shape
    scale_factor = float(tok_count * devices) ** (-0.5)
    rows = branches * piece
    f32 = jnp.float32
    dma = pltpu.SemaphoreType.DMA
    weight_t = jnp.transpose(proj_weight, (1, 2, 3, 0))
    own, signals = pl.pallas_call(
        functools.partial(gather_kernel, devices, count),
        out_shape=(
            jax.ShapeDtypeStruct((rows, vocabulary), f32),
            jax.ShapeDtypeStruct((devices, 2 * piece + 8, tok_count), f32),
        ),
        in_specs=[VMEM] * 5,
        out_specs=(VMEM, VMEM),
        scratch_shapes=[
            pltpu.VMEM((count, rows, vocabulary), f32),
            pltpu.VMEM((count, rows, vocabulary), f32),
            pltpu.VMEM((count, rows, vocabulary), f32),
            pltpu.VMEM((devices, 2 * piece + 8, tok_count), f32),
            dma((devices - 1,)),
            dma((devices - 1,)),
            dma((count,)),
            dma((count,)),
            dma((count,)),
            dma((count,)),
        ],
        compiler_params=pltpu.CompilerParams(collective_id=0, has_side_effects=True),
        name="gather_signals",
    )(token_ids.reshape(1, tok_count), embedding, weight_t, filters, cotangent)
    high, low = transform_tables(tok_count, devices)
    sending, sums = pl.pallas_call(
        functools.partial(middle_kernel, scale_factor),
        out_shape=(
            jax.ShapeDtypeStruct((devices, 5 * piece, tok_count), f32),
            jax.ShapeDtypeStruct((rows, vocabulary), f32),
        ),
        in_specs=[VMEM] * 4,
        out_specs=(VMEM, VMEM),
        name="convolve_channels",
    )(own, signals, jnp.asarray(high), jnp.asarray(low))
    received, all_sums = pl.pallas_call(
        functools.partial(return_kernel, devices, count),
        out_shape=(
            jax.ShapeDtypeStruct((devices, 5 * piece, tok_count), f32),
            jax.ShapeDtypeStruct((count, rows, vocabulary), f32),
        ),
        in_specs=[VMEM] * 2,
        out_specs=(VMEM, VMEM),
        scratch_shapes=[
            dma((devices - 1,)),
            dma((devices - 1,)),
            dma((count,)),
            dma((count,)),
            dma((count,)),
            dma((count,)),
        ],
        compiler_params=pltpu.CompilerParams(collective_id=1, has_side_effects=True),
        name="return_results",
    )(sending, sums)
    output, filter_grad, grads, weight = pl.pallas_call(
        functools.partial(final_kernel, scale_factor),
        out_shape=(
            jax.ShapeDtypeStruct((tok_count, width), f32),
            jax.ShapeDtypeStruct((tok_count, width), f32),
            jax.ShapeDtypeStruct((branches, tok_count, width), jnp.bfloat16),
            jax.ShapeDtypeStruct((branches, count, piece, depth), f32),
        ),
        in_specs=[VMEM] * 3,
        out_specs=(VMEM,) * 4,
        name="finish",
    )(embedding, received, all_sums)
    return (
        output,
        filter_grad,
        jnp.transpose(grads, (1, 0, 2)),
        jnp.transpose(weight, (3, 0, 1, 2)),
    )


def fits_kernels(devices, count, token_ids, embedding, proj_weight, filters):
    tok_count, width = filters.shape
    vocabulary, depth = embedding.shape
    _, branches, red_count, piece = proj_weight.shape
    lanes = (tok_count, vocabulary, depth)
    aligned = all(size % 128 == 0 for size in lanes) and piece % 16 == 0
    tables = devices * (2 * tok_count) ** 2 * 4
    one_hot = vocabulary * tok_count * devices * 8
    held = 4 * branches * piece * vocabulary * (3 * count + 2)
    return (
        aligned
        and branches == 3
        and red_count == count
        and width == devices * piece
        and tables + one_hot + held < 40 * 2**20
    )


def angles(numbers, modulus, direction):
    phase = (numbers % modulus).astype(jnp.float32) * (direction * 2.0 * math.pi / modulus)
    return (jnp.cos(phase), jnp.sin(phase))


def rotate(real_part, imag_part, cosine, sine_part):
    return (real_part * cosine - imag_part * sine_part, real_part * sine_part + imag_part * cosine)


def complex_einsum(formula, matrix, values):
    mat_real, mat_imag = matrix
    val_real, val_imag = values
    real_out = jnp.einsum(formula, mat_real, val_real, precision=precise_mode) - jnp.einsum(
        formula, mat_imag, val_imag, precision=precise_mode
    )
    imag_out = jnp.einsum(formula, mat_real, val_imag, precision=precise_mode) + jnp.einsum(
        formula, mat_imag, val_real, precision=precise_mode
    )
    return (real_out, imag_out)


def factors(length_total):
    first_factor = 1
    for candidate in range(1, math.isqrt(length_total) + 1):
        if length_total % candidate == 0:
            first_factor = candidate
    return (first_factor, length_total // first_factor)


def combine_spectra(spec_real, spec_imag, width):
    filt_re = spec_real[..., :width]
    inner_re = spec_real[..., width : 2 * width]
    up_re = spec_real[..., 2 * width :]
    filt_im = spec_imag[..., :width]
    inner_im = spec_imag[..., width : 2 * width]
    up_im = spec_imag[..., 2 * width :]
    joined_real = jnp.concatenate(
        [
            filt_re * inner_re - filt_im * inner_im,
            filt_re * up_re + filt_im * up_im,
            up_re * inner_re + up_im * inner_im,
        ],
        axis=-1,
    )
    joined_imag = jnp.concatenate(
        [
            filt_re * inner_im + filt_im * inner_re,
            filt_re * up_im - filt_im * up_re,
            up_im * inner_re - up_re * inner_im,
        ],
        axis=-1,
    )
    return (joined_real, joined_imag)


def local_convolve(signals):
    length, branch_count, narrow = signals.shape
    total = 2 * length
    first_factor, second_factor = factors(total)
    flat = signals.reshape(length, branch_count * narrow)
    padded = jnp.concatenate([flat, jnp.zeros_like(flat)], axis=0).reshape(
        first_factor, second_factor, branch_count * narrow
    )
    first_index = jnp.arange(first_factor, dtype=jnp.int32)
    second_index = jnp.arange(second_factor, dtype=jnp.int32)
    cosine, sine_part = angles(first_index[:, None] * first_index[None, :], first_factor, -1.0)
    real_part = jnp.einsum("kn,nbm->kbm", cosine, padded, precision=precise_mode)
    imag_part = jnp.einsum("kn,nbm->kbm", sine_part, padded, precision=precise_mode)
    cosine, sine_part = angles(first_index[:, None] * second_index[None, :], total, -1.0)
    real_part, imag_part = rotate(real_part, imag_part, cosine[:, :, None], sine_part[:, :, None])
    real_part, imag_part = complex_einsum(
        "lb,kbm->klm",
        angles(second_index[:, None] * second_index[None, :], second_factor, -1.0),
        (real_part, imag_part),
    )
    real_part, imag_part = combine_spectra(real_part, imag_part, narrow)
    real_part, imag_part = complex_einsum(
        "bl,klm->kbm",
        angles(second_index[:, None] * second_index[None, :], second_factor, 1.0),
        (real_part, imag_part),
    )
    cosine, sine_part = angles(first_index[:, None] * second_index[None, :], total, 1.0)
    real_part, imag_part = rotate(real_part, imag_part, cosine[:, :, None], sine_part[:, :, None])
    cosine, sine_part = angles(first_index[:, None] * first_index[None, :], first_factor, 1.0)
    result = jnp.einsum("nk,kbm->nbm", cosine, real_part, precision=precise_mode) - jnp.einsum(
        "nk,kbm->nbm", sine_part, imag_part, precision=precise_mode
    )
    result = result.reshape(total, branch_count * narrow)[:length] / total
    return result.reshape(length, branch_count, narrow)


def shards(token_ids, embedding, proj_weight, filters, cotangent):
    tok_count = token_ids.shape[0]
    devices = lax.axis_size("seq")
    count = lax.axis_size("red")
    if fits_kernels(devices, count, token_ids, embedding, proj_weight, filters):
        return kernel_shards(
            devices, count, token_ids, embedding, proj_weight, filters, cotangent
        )
    width = filters.shape[1]
    vocabulary = embedding.shape[0]
    width_rows, branches, red_count, piece = proj_weight.shape
    scale_factor = float(tok_count * devices) ** (-0.5)
    table = jnp.dot(
        embedding,
        proj_weight.reshape(width_rows, branches * red_count * piece),
        preferred_element_type=jnp.float32,
    )
    table = table.reshape(vocabulary, branches, red_count, piece)
    own_table = lax.psum_scatter(table, "red", scatter_dimension=2, tiled=True)
    full_table = lax.all_gather(own_table, "seq", axis=3, tiled=True)
    projected = jnp.take(full_table, token_ids, axis=0)
    projected = projected.reshape(tok_count, branches, width)
    queries = projected[:, 0]
    key_rows = projected[:, 1]
    value_rows = projected[:, 2]
    inner = key_rows * value_rows
    upstream = cotangent * queries
    stacked = jnp.stack([filters, inner, upstream], axis=1)
    whole_length = lax.all_to_all(stacked, "seq", split_axis=2, concat_axis=0, tiled=True)
    results = local_convolve(whole_length)
    returned = lax.all_to_all(results, "seq", split_axis=0, concat_axis=2, tiled=True)
    conv = returned[:, 0]
    grad_inner = returned[:, 1]
    filter_raw = returned[:, 2]
    output = queries * conv
    filter_grad = filter_raw * scale_factor
    branch_grads = jnp.stack(
        [cotangent * conv, grad_inner * value_rows, grad_inner * key_rows], axis=1
    ).astype(jnp.bfloat16)
    one_hot = (token_ids[:, None] == lax.iota(jnp.int32, vocabulary)[None, :]).astype(jnp.bfloat16)
    token_sums = lax.dot_general(
        one_hot,
        branch_grads.reshape(tok_count, branches * width),
        (((0,), (0,)), ((), ())),
        preferred_element_type=jnp.float32,
    )
    summed = lax.psum_scatter(
        token_sums.reshape(vocabulary, branches, width), "seq", scatter_dimension=2, tiled=True
    )
    gathered = lax.all_gather(summed[:, :, None, :], "red", axis=2, tiled=True)
    weight_grad = (
        lax.dot_general(
            embedding.astype(jnp.float32),
            gathered.reshape(vocabulary, branches * red_count * piece),
            (((0,), (0,)), ((), ())),
            precision=precise_mode,
        )
        * scale_factor
    )
    return (
        output,
        filter_grad,
        branch_grads,
        weight_grad.reshape(width_rows, branches, red_count, piece),
    )


def solution(mesh):
    in_specs = (
        P("seq"),
        P(None, "red"),
        P("red", None, None, "seq"),
        P("seq", "red"),
        P("seq", "red"),
    )
    out_specs = (
        P("seq", "red"),
        P("seq", "red"),
        P("seq", None, "red"),
        P("red", None, None, "seq"),
    )
    return jax.shard_map(shards, mesh=mesh, in_specs=in_specs, out_specs=out_specs, check_vma=False)
```

```python
import functools
import math

import jax
import jax.numpy as jnp
import numpy as np
from jax import lax
from jax.experimental import pallas as pl
from jax.experimental.pallas import tpu as pltpu
from jax.sharding import PartitionSpec as P

precise_mode = lax.Precision.HIGHEST
MESH = pl.DeviceIdType.MESH
VMEM = pl.BlockSpec(memory_space=pltpu.VMEM)
NN = (((1,), (0,)), ((), ()))
NT = (((1,), (1,)), ((), ()))


def split(value):
    high = value.astype(jnp.bfloat16)
    low = (value - high.astype(jnp.float32)).astype(jnp.bfloat16)
    return high, low


def dot(left, right, dims=NN):
    return lax.dot_general(left, right, dims, preferred_element_type=jnp.float32)


def dot_split(value, matrix, dims=NN):
    high, low = split(value)
    both = dot(jnp.concatenate([high, low], axis=0), matrix, dims)
    rows = value.shape[0]
    return both[:rows] + both[rows:]


def dot_both(value, matrix_high, matrix_low, dims=NN):
    high, _ = split(value)
    return dot_split(value, matrix_high, dims) + dot(high, matrix_low, dims)


def transform_tables(block, blocks):
    total = 2 * blocks * block
    place = np.arange(block)
    half = block // 2
    tables = np.zeros((blocks, 2 * block, 2 * block))
    even = 2 * np.pi * ((2 * blocks * place[:, None] * np.arange(half)[None, :]) % total) / total
    odd = 2 * np.pi * ((place[:, None] * (blocks + 2 * blocks * np.arange(half))[None, :]) % total) / total
    tables[0, :block, :half] = np.cos(even)
    tables[0, :block, block : block + half] = np.sin(even)
    tables[0, :block, block] = 1.0 - 2.0 * (place % 2)
    tables[0, block:, half:block] = np.cos(odd)
    tables[0, block:, block + half :] = np.sin(odd)
    for residue in range(1, blocks):
        freq = residue + 2 * blocks * np.arange(block)
        psi = 2 * np.pi * ((place[:, None] * freq[None, :]) % total) / total
        tables[residue, :block, :block] = np.cos(psi)
        tables[residue, :block, block:] = np.sin(psi)
        tables[residue, block:, :block] = -np.sin(psi)
        tables[residue, block:, block:] = np.cos(psi)
    tables = tables.astype(np.float32)
    high = tables.astype(jnp.bfloat16)
    low = (tables - high.astype(np.float32)).astype(jnp.bfloat16)
    return high, low


def phases(residue, blocks):
    if residue == 0:
        return [1.0] * blocks, [(-1.0) ** index for index in range(blocks)]
    turn = [math.pi * ((residue * index) % (2 * blocks)) / blocks for index in range(blocks)]
    return [math.cos(a) for a in turn], [math.sin(a) for a in turn]


def weighted(terms, weights):
    total = None
    for term, weight in zip(terms, weights):
        if abs(weight) < 1e-12:
            continue
        part = term if weight == 1.0 else term * weight
        total = part if total is None else total + part
    return total


def greet(devices, count):
    me = lax.axis_index("seq")
    spot = lax.axis_index("red")
    barrier = pltpu.get_barrier_semaphore()
    for step in range(1, devices):
        peer = lax.rem(me + step, devices)
        pl.semaphore_signal(barrier, inc=1, device_id={"seq": peer}, device_id_type=MESH)

    @pl.when(spot > 0)
    def _():
        pl.semaphore_signal(barrier, inc=1, device_id={"red": spot - 1}, device_id_type=MESH)

    @pl.when(spot < count - 1)
    def _():
        pl.semaphore_signal(barrier, inc=1, device_id={"red": spot + 1}, device_id_type=MESH)

    neighbours = jnp.where(spot > 0, 1, 0) + jnp.where(spot < count - 1, 1, 0)
    pl.semaphore_wait(barrier, devices - 1 + neighbours)


def exchange(devices, source, target, send_sem, recv_sem):
    me = lax.axis_index("seq")
    copies = []
    for step in range(1, devices):
        peer = lax.rem(me + step, devices)
        copy = pltpu.make_async_remote_copy(
            src_ref=source.at[peer],
            dst_ref=target.at[me],
            send_sem=send_sem.at[step - 1],
            recv_sem=recv_sem.at[step - 1],
            device_id={"seq": peer},
            device_id_type=MESH,
        )
        copy.start()
        copies.append(copy)
    return copies


def gather_kernel(
    devices, count, tok_ref, emb_ref, wt_ref, filt_ref, cot_ref,
    own_ref, sig_ref,
    part, from_left, from_right, out_sig,
    send_sig, recv_sig, send_right, recv_right, send_left, recv_left,
):
    me = lax.axis_index("seq")
    spot = lax.axis_index("red")
    branches, _, piece, _ = wt_ref.shape
    tok_count, width = filt_ref.shape
    filt_t = filt_ref[...].T
    cot_t = cot_ref[...].T
    tok_rows = jnp.broadcast_to(tok_ref[...].astype(jnp.float32), (8, tok_count))
    for peer in range(devices):
        out_sig[peer, :piece] = filt_t[peer * piece : (peer + 1) * piece]
        out_sig[peer, piece : 2 * piece] = cot_t[peer * piece : (peer + 1) * piece]
        out_sig[peer, 2 * piece :] = tok_rows
    greet(devices, count)
    copies = exchange(devices, out_sig, sig_ref, send_sig, recv_sig)
    table = emb_ref[...]
    for group in range(count):
        rows = jnp.concatenate([wt_ref[branch, group] for branch in range(branches)], axis=0)
        part[group] = dot(rows, table, NT)
    sig_ref[me] = out_sig[me]

    def hop(slot, target, sends, recvs, neighbour):
        return pltpu.make_async_remote_copy(
            src_ref=part.at[slot],
            dst_ref=target.at[slot],
            send_sem=sends.at[slot],
            recv_sem=recvs.at[slot],
            device_id={"red": neighbour},
            device_id_type=MESH,
        )

    right = functools.partial(
        hop, target=from_left, sends=send_right, recvs=recv_right,
        neighbour=jnp.minimum(spot + 1, count - 1),
    )
    left = functools.partial(
        hop, target=from_right, sends=send_left, recvs=recv_left,
        neighbour=jnp.maximum(spot - 1, 0),
    )
    for tick in range(2 * count - 2):
        goal = count - 1 - (tick - spot)

        @pl.when((tick >= spot) & (spot < goal))
        def _():
            @pl.when(spot > 0)
            def _():
                right(goal).wait_recv()
                part[goal] = part[goal] + from_left[goal]

            right(goal).start()

        other = tick - (count - 1 - spot)

        @pl.when((other >= 0) & (spot > other))
        def _():
            @pl.when(spot < count - 1)
            def _():
                left(other).wait_recv()
                part[other] = part[other] + from_right[other]

            left(other).start()

    for goal in range(count):
        @pl.when(spot == goal)
        def _():
            total = part[goal]
            if goal > 0:
                right(goal).wait_recv()
                total = total + from_left[goal]
            if goal < count - 1:
                left(goal).wait_recv()
                total = total + from_right[goal]
            own_ref[...] = total

        @pl.when(spot < goal)
        def _():
            right(goal).wait_send()

        @pl.when(spot > goal)
        def _():
            left(goal).wait_send()

    for copy in copies:
        copy.wait()


def convolve(signals, high_ref, low_ref, piece):
    blocks, double, _ = high_ref.shape
    block = double // 2
    pieces = [signals[:, index * block : (index + 1) * block] for index in range(blocks)]
    results = [None] * blocks
    scale = 1.0 / (blocks * block)
    for residue in range(blocks):
        cosines, sines = phases(residue, blocks)
        packed = jnp.concatenate([weighted(pieces, cosines), weighted(pieces, sines)], axis=1)
        spectrum = dot_both(packed, high_ref[residue], low_ref[residue])
        cos_part = spectrum[:, :block]
        sin_part = spectrum[:, block:]
        fc, ic, uc = (cos_part[at * piece : (at + 1) * piece] for at in range(3))
        fs, i_s, us = (sin_part[at * piece : (at + 1) * piece] for at in range(3))
        cc = [fc * ic, fc * uc, uc * ic]
        ss = [fs * i_s, fs * us, us * i_s]
        signs = [-1.0, 1.0, 1.0]
        new_cos = [c + sign * s for c, s, sign in zip(cc, ss, signs)]
        new_sin = [fc * i_s + fs * ic, fc * us - fs * uc, us * ic - uc * i_s]
        new_cos = jnp.concatenate(new_cos, axis=0)
        new_sin = jnp.concatenate(new_sin, axis=0)
        if residue == 0:
            first = lax.broadcasted_iota(jnp.int32, new_cos.shape, 1) == 0
            new_cos = jnp.where(first, 0.5 * jnp.concatenate(cc, axis=0), new_cos)
            new_sin = jnp.where(first, 0.5 * jnp.concatenate(ss, axis=0), new_sin)
        joined = jnp.concatenate([new_cos, new_sin], axis=1) * scale
        back = dot_both(joined, high_ref[residue], low_ref[residue], NT)
        first_half = back[:, :block]
        second_half = back[:, block:]
        for index in range(blocks):
            term = weighted([first_half, second_half], [cosines[index], sines[index]])
            results[index] = term if results[index] is None else results[index] + term
    return results


def middle_kernel(scale_factor, own_ref, sig_ref, high_ref, low_ref, send_ref, sums_ref):
    vocabulary = own_ref.shape[1]
    devices, _, block = sig_ref.shape
    piece = own_ref.shape[0] // 3
    ids = jnp.concatenate([sig_ref[at, 2 * piece : 2 * piece + 1] for at in range(devices)], axis=1)
    length = devices * block
    rows = lax.broadcasted_iota(jnp.int32, (vocabulary, length), 0)
    one_hot = jnp.where(rows == ids.astype(jnp.int32), 1.0, 0.0).astype(jnp.bfloat16)
    projected = dot_split(own_ref[...], one_hot)
    queries = projected[:piece]
    key_rows = projected[piece : 2 * piece]
    value_rows = projected[2 * piece :]
    filters = jnp.concatenate([sig_ref[at, :piece] for at in range(devices)], axis=1)
    cotangent = jnp.concatenate([sig_ref[at, piece : 2 * piece] for at in range(devices)], axis=1)
    signals = jnp.concatenate([filters, key_rows * value_rows, cotangent * queries], axis=0)
    results = convolve(signals, high_ref, low_ref, piece)
    rounded = []
    for at in range(devices):
        lanes = slice(at * block, (at + 1) * block)
        conv = results[at][:piece]
        grad_inner = results[at][piece : 2 * piece]
        grads = jnp.concatenate(
            [
                cotangent[:, lanes] * conv,
                grad_inner * value_rows[:, lanes],
                grad_inner * key_rows[:, lanes],
            ],
            axis=0,
        ).astype(jnp.bfloat16)
        rounded.append(grads)
        send_ref[at, :piece] = queries[:, lanes] * conv
        send_ref[at, piece : 2 * piece] = results[at][2 * piece :] * scale_factor
        send_ref[at, 2 * piece :] = grads.astype(jnp.float32)
    sums_ref[...] = dot(jnp.concatenate(rounded, axis=1), one_hot, NT)


def return_kernel(
    devices, count, send_ref, sums_ref, recv_ref, all_ref,
    send_sem, recv_sem, send_right, recv_right, send_left, recv_left,
):
    me = lax.axis_index("seq")
    spot = lax.axis_index("red")
    greet(devices, count)

    def hop(source, slot, sends, recvs, neighbour):
        return pltpu.make_async_remote_copy(
            src_ref=source,
            dst_ref=all_ref.at[slot],
            send_sem=sends.at[slot],
            recv_sem=recvs.at[slot],
            device_id={"red": neighbour},
            device_id_type=MESH,
        )

    def right(source, slot):
        return hop(source, slot, send_right, recv_right, jnp.minimum(spot + 1, count - 1))

    def left(source, slot):
        return hop(source, slot, send_left, recv_left, jnp.maximum(spot - 1, 0))

    @pl.when(spot < count - 1)
    def _():
        right(sums_ref, spot).start()

    @pl.when(spot > 0)
    def _():
        left(sums_ref, spot).start()

    copies = exchange(devices, send_ref, recv_ref, send_sem, recv_sem)
    all_ref[spot] = sums_ref[...]
    recv_ref[me] = send_ref[me]
    for step in range(1, count):
        below = spot - step

        @pl.when(below >= 0)
        def _():
            right(all_ref.at[below], below).wait_recv()

            @pl.when(spot < count - 1)
            def _():
                right(all_ref.at[below], below).start()

        above = spot + step

        @pl.when(above < count)
        def _():
            left(all_ref.at[above], above).wait_recv()

            @pl.when(spot > 0)
            def _():
                left(all_ref.at[above], above).start()

    for step in range(count):
        @pl.when((spot - step >= 0) & (spot < count - 1))
        def _():
            right(sums_ref, spot - step).wait_send()

        @pl.when((spot + step < count) & (spot > 0))
        def _():
            left(sums_ref, spot + step).wait_send()

    for copy in copies:
        copy.wait()


def final_kernel(scale_factor, emb_ref, recv_ref, all_ref, out_ref, filt_ref, grads_ref, weight_ref):
    devices, rows, _ = recv_ref.shape
    piece = rows // 5
    count = all_ref.shape[0]
    table = emb_ref[...]
    for group in range(count):
        product = dot_split(all_ref[group], table) * scale_factor
        for branch in range(3):
            weight_ref[branch, group] = product[branch * piece : (branch + 1) * piece]

    def positions(at):
        parts = [recv_ref[peer, at * piece : (at + 1) * piece] for peer in range(devices)]
        return jnp.concatenate(parts, axis=0).T

    out_ref[...] = positions(0)
    filt_ref[...] = positions(1)
    for branch in range(3):
        grads_ref[branch] = positions(2 + branch).astype(jnp.bfloat16)


def kernel_shards(devices, count, token_ids, embedding, proj_weight, filters, cotangent):
    tok_count, width = filters.shape
    vocabulary, depth = embedding.shape
    _, branches, _, piece = proj_weight.shape
    scale_factor = float(tok_count * devices) ** (-0.5)
    rows = branches * piece
    f32 = jnp.float32
    dma = pltpu.SemaphoreType.DMA
    weight_t = jnp.transpose(proj_weight, (1, 2, 3, 0))
    own, signals = pl.pallas_call(
        functools.partial(gather_kernel, devices, count),
        out_shape=(
            jax.ShapeDtypeStruct((rows, vocabulary), f32),
            jax.ShapeDtypeStruct((devices, 2 * piece + 8, tok_count), f32),
        ),
        in_specs=[VMEM] * 5,
        out_specs=(VMEM, VMEM),
        scratch_shapes=[
            pltpu.VMEM((count, rows, vocabulary), f32),
            pltpu.VMEM((count, rows, vocabulary), f32),
            pltpu.VMEM((count, rows, vocabulary), f32),
            pltpu.VMEM((devices, 2 * piece + 8, tok_count), f32),
            dma((devices - 1,)),
            dma((devices - 1,)),
            dma((count,)),
            dma((count,)),
            dma((count,)),
            dma((count,)),
        ],
        compiler_params=pltpu.CompilerParams(collective_id=0, has_side_effects=True),
        name="gather_signals",
    )(token_ids.reshape(1, tok_count), embedding, weight_t, filters, cotangent)
    high, low = transform_tables(tok_count, devices)
    sending, sums = pl.pallas_call(
        functools.partial(middle_kernel, scale_factor),
        out_shape=(
            jax.ShapeDtypeStruct((devices, 5 * piece, tok_count), f32),
            jax.ShapeDtypeStruct((rows, vocabulary), f32),
        ),
        in_specs=[VMEM] * 4,
        out_specs=(VMEM, VMEM),
        name="convolve_channels",
    )(own, signals, jnp.asarray(high), jnp.asarray(low))
    received, all_sums = pl.pallas_call(
        functools.partial(return_kernel, devices, count),
        out_shape=(
            jax.ShapeDtypeStruct((devices, 5 * piece, tok_count), f32),
            jax.ShapeDtypeStruct((count, rows, vocabulary), f32),
        ),
        in_specs=[VMEM] * 2,
        out_specs=(VMEM, VMEM),
        scratch_shapes=[
            dma((devices - 1,)),
            dma((devices - 1,)),
            dma((count,)),
            dma((count,)),
            dma((count,)),
            dma((count,)),
        ],
        compiler_params=pltpu.CompilerParams(collective_id=1, has_side_effects=True),
        name="return_results",
    )(sending, sums)
    output, filter_grad, grads, weight = pl.pallas_call(
        functools.partial(final_kernel, scale_factor),
        out_shape=(
            jax.ShapeDtypeStruct((tok_count, width), f32),
            jax.ShapeDtypeStruct((tok_count, width), f32),
            jax.ShapeDtypeStruct((branches, tok_count, width), jnp.bfloat16),
            jax.ShapeDtypeStruct((branches, count, piece, depth), f32),
        ),
        in_specs=[VMEM] * 3,
        out_specs=(VMEM,) * 4,
        name="finish",
    )(embedding, received, all_sums)
    return (
        output,
        filter_grad,
        jnp.transpose(grads, (1, 0, 2)),
        jnp.transpose(weight, (3, 0, 1, 2)),
    )


def fits_kernels(devices, count, token_ids, embedding, proj_weight, filters):
    tok_count, width = filters.shape
    vocabulary, depth = embedding.shape
    _, branches, red_count, piece = proj_weight.shape
    lanes = (tok_count, vocabulary, depth)
    aligned = all(size % 128 == 0 for size in lanes) and piece % 16 == 0
    tables = devices * (2 * tok_count) ** 2 * 4
    one_hot = vocabulary * tok_count * devices * 8
    held = 4 * branches * piece * vocabulary * (3 * count + 2)
    return (
        aligned
        and branches == 3
        and red_count == count
        and width == devices * piece
        and tables + one_hot + held < 40 * 2**20
    )


def angles(numbers, modulus, direction):
    phase = (numbers % modulus).astype(jnp.float32) * (direction * 2.0 * math.pi / modulus)
    return (jnp.cos(phase), jnp.sin(phase))


def rotate(real_part, imag_part, cosine, sine_part):
    return (real_part * cosine - imag_part * sine_part, real_part * sine_part + imag_part * cosine)


def complex_einsum(formula, matrix, values):
    mat_real, mat_imag = matrix
    val_real, val_imag = values
    real_out = jnp.einsum(formula, mat_real, val_real, precision=precise_mode) - jnp.einsum(
        formula, mat_imag, val_imag, precision=precise_mode
    )
    imag_out = jnp.einsum(formula, mat_real, val_imag, precision=precise_mode) + jnp.einsum(
        formula, mat_imag, val_real, precision=precise_mode
    )
    return (real_out, imag_out)


def factors(length_total):
    first_factor = 1
    for candidate in range(1, math.isqrt(length_total) + 1):
        if length_total % candidate == 0:
            first_factor = candidate
    return (first_factor, length_total // first_factor)


def combine_spectra(spec_real, spec_imag, width):
    filt_re = spec_real[..., :width]
    inner_re = spec_real[..., width : 2 * width]
    up_re = spec_real[..., 2 * width :]
    filt_im = spec_imag[..., :width]
    inner_im = spec_imag[..., width : 2 * width]
    up_im = spec_imag[..., 2 * width :]
    joined_real = jnp.concatenate(
        [
            filt_re * inner_re - filt_im * inner_im,
            filt_re * up_re + filt_im * up_im,
            up_re * inner_re + up_im * inner_im,
        ],
        axis=-1,
    )
    joined_imag = jnp.concatenate(
        [
            filt_re * inner_im + filt_im * inner_re,
            filt_re * up_im - filt_im * up_re,
            up_im * inner_re - up_re * inner_im,
        ],
        axis=-1,
    )
    return (joined_real, joined_imag)


def local_convolve(signals):
    length, branch_count, narrow = signals.shape
    total = 2 * length
    first_factor, second_factor = factors(total)
    flat = signals.reshape(length, branch_count * narrow)
    padded = jnp.concatenate([flat, jnp.zeros_like(flat)], axis=0).reshape(
        first_factor, second_factor, branch_count * narrow
    )
    first_index = jnp.arange(first_factor, dtype=jnp.int32)
    second_index = jnp.arange(second_factor, dtype=jnp.int32)
    cosine, sine_part = angles(first_index[:, None] * first_index[None, :], first_factor, -1.0)
    real_part = jnp.einsum("kn,nbm->kbm", cosine, padded, precision=precise_mode)
    imag_part = jnp.einsum("kn,nbm->kbm", sine_part, padded, precision=precise_mode)
    cosine, sine_part = angles(first_index[:, None] * second_index[None, :], total, -1.0)
    real_part, imag_part = rotate(real_part, imag_part, cosine[:, :, None], sine_part[:, :, None])
    real_part, imag_part = complex_einsum(
        "lb,kbm->klm",
        angles(second_index[:, None] * second_index[None, :], second_factor, -1.0),
        (real_part, imag_part),
    )
    real_part, imag_part = combine_spectra(real_part, imag_part, narrow)
    real_part, imag_part = complex_einsum(
        "bl,klm->kbm",
        angles(second_index[:, None] * second_index[None, :], second_factor, 1.0),
        (real_part, imag_part),
    )
    cosine, sine_part = angles(first_index[:, None] * second_index[None, :], total, 1.0)
    real_part, imag_part = rotate(real_part, imag_part, cosine[:, :, None], sine_part[:, :, None])
    cosine, sine_part = angles(first_index[:, None] * first_index[None, :], first_factor, 1.0)
    result = jnp.einsum("nk,kbm->nbm", cosine, real_part, precision=precise_mode) - jnp.einsum(
        "nk,kbm->nbm", sine_part, imag_part, precision=precise_mode
    )
    result = result.reshape(total, branch_count * narrow)[:length] / total
    return result.reshape(length, branch_count, narrow)


def shards(token_ids, embedding, proj_weight, filters, cotangent):
    tok_count = token_ids.shape[0]
    devices = lax.axis_size("seq")
    count = lax.axis_size("red")
    if fits_kernels(devices, count, token_ids, embedding, proj_weight, filters):
        return kernel_shards(
            devices, count, token_ids, embedding, proj_weight, filters, cotangent
        )
    width = filters.shape[1]
    vocabulary = embedding.shape[0]
    width_rows, branches, red_count, piece = proj_weight.shape
    scale_factor = float(tok_count * devices) ** (-0.5)
    table = jnp.dot(
        embedding,
        proj_weight.reshape(width_rows, branches * red_count * piece),
        preferred_element_type=jnp.float32,
    )
    table = table.reshape(vocabulary, branches, red_count, piece)
    own_table = lax.psum_scatter(table, "red", scatter_dimension=2, tiled=True)
    full_table = lax.all_gather(own_table, "seq", axis=3, tiled=True)
    projected = jnp.take(full_table, token_ids, axis=0)
    projected = projected.reshape(tok_count, branches, width)
    queries = projected[:, 0]
    key_rows = projected[:, 1]
    value_rows = projected[:, 2]
    inner = key_rows * value_rows
    upstream = cotangent * queries
    stacked = jnp.stack([filters, inner, upstream], axis=1)
    whole_length = lax.all_to_all(stacked, "seq", split_axis=2, concat_axis=0, tiled=True)
    results = local_convolve(whole_length)
    returned = lax.all_to_all(results, "seq", split_axis=0, concat_axis=2, tiled=True)
    conv = returned[:, 0]
    grad_inner = returned[:, 1]
    filter_raw = returned[:, 2]
    output = queries * conv
    filter_grad = filter_raw * scale_factor
    branch_grads = jnp.stack(
        [cotangent * conv, grad_inner * value_rows, grad_inner * key_rows], axis=1
    ).astype(jnp.bfloat16)
    one_hot = (token_ids[:, None] == lax.iota(jnp.int32, vocabulary)[None, :]).astype(jnp.bfloat16)
    token_sums = lax.dot_general(
        one_hot,
        branch_grads.reshape(tok_count, branches * width),
        (((0,), (0,)), ((), ())),
        preferred_element_type=jnp.float32,
    )
    summed = lax.psum_scatter(
        token_sums.reshape(vocabulary, branches, width), "seq", scatter_dimension=2, tiled=True
    )
    gathered = lax.all_gather(summed[:, :, None, :], "red", axis=2, tiled=True)
    weight_grad = (
        lax.dot_general(
            embedding.astype(jnp.float32),
            gathered.reshape(vocabulary, branches * red_count * piece),
            (((0,), (0,)), ((), ())),
            precision=precise_mode,
        )
        * scale_factor
    )
    return (
        output,
        filter_grad,
        branch_grads,
        weight_grad.reshape(width_rows, branches, red_count, piece),
    )


def solution(mesh):
    in_specs = (
        P("seq"),
        P(None, "red"),
        P("red", None, None, "seq"),
        P("seq", "red"),
        P("seq", "red"),
    )
    out_specs = (
        P("seq", "red"),
        P("seq", "red"),
        P("seq", None, "red"),
        P("red", None, None, "seq"),
    )
    return jax.shard_map(shards, mesh=mesh, in_specs=in_specs, out_specs=out_specs, check_vma=False)
```

```python
import functools
import math

import jax
import jax.numpy as jnp
import numpy as np
from jax import lax
from jax.experimental import pallas as pl
from jax.experimental.pallas import tpu as pltpu
from jax.sharding import PartitionSpec as P

precise_mode = lax.Precision.HIGHEST
MESH = pl.DeviceIdType.MESH
VMEM = pl.BlockSpec(memory_space=pltpu.VMEM)
CHUNKS = 2
NN = (((1,), (0,)), ((), ()))
NT = (((1,), (1,)), ((), ()))


def split(value):
    high = value.astype(jnp.bfloat16)
    low = (value - high.astype(jnp.float32)).astype(jnp.bfloat16)
    return high, low


def dot(left, right, dims=NN):
    return lax.dot_general(left, right, dims, preferred_element_type=jnp.float32)


def dot_split(value, matrix, dims=NN):
    high, low = split(value)
    both = dot(jnp.concatenate([high, low], axis=0), matrix, dims)
    rows = value.shape[0]
    return both[:rows] + both[rows:]


def dot_both(value, matrix_high, matrix_low, dims=NN):
    high, _ = split(value)
    return dot_split(value, matrix_high, dims) + dot(high, matrix_low, dims)


def transform_tables(block, blocks):
    total = 2 * blocks * block
    place = np.arange(block)
    half = block // 2
    tables = np.zeros((blocks, 2 * block, 2 * block))
    even = 2 * np.pi * ((2 * blocks * place[:, None] * np.arange(half)[None, :]) % total) / total
    odd = 2 * np.pi * ((place[:, None] * (blocks + 2 * blocks * np.arange(half))[None, :]) % total) / total
    tables[0, :block, :half] = np.cos(even)
    tables[0, :block, block : block + half] = np.sin(even)
    tables[0, :block, block] = 1.0 - 2.0 * (place % 2)
    tables[0, block:, half:block] = np.cos(odd)
    tables[0, block:, block + half :] = np.sin(odd)
    for residue in range(1, blocks):
        freq = residue + 2 * blocks * np.arange(block)
        psi = 2 * np.pi * ((place[:, None] * freq[None, :]) % total) / total
        tables[residue, :block, :block] = np.cos(psi)
        tables[residue, :block, block:] = np.sin(psi)
        tables[residue, block:, :block] = -np.sin(psi)
        tables[residue, block:, block:] = np.cos(psi)
    tables = tables.astype(np.float32)
    high = tables.astype(jnp.bfloat16)
    low = (tables - high.astype(np.float32)).astype(jnp.bfloat16)
    return high, low


def phases(residue, blocks):
    if residue == 0:
        return [1.0] * blocks, [(-1.0) ** index for index in range(blocks)]
    turn = [math.pi * ((residue * index) % (2 * blocks)) / blocks for index in range(blocks)]
    return [math.cos(a) for a in turn], [math.sin(a) for a in turn]


def weighted(terms, weights):
    total = None
    for term, weight in zip(terms, weights):
        if abs(weight) < 1e-12:
            continue
        part = term if weight == 1.0 else term * weight
        total = part if total is None else total + part
    return total


def convolve(signals, high_ref, low_ref, piece, beside):
    blocks, double, _ = high_ref.shape
    block = double // 2
    pieces = [signals[:, index * block : (index + 1) * block] for index in range(blocks)]
    results = [None] * blocks
    scale = 1.0 / (blocks * block)
    for residue in range(blocks):
        if residue == blocks // 2:
            beside()
        cosines, sines = phases(residue, blocks)
        packed = jnp.concatenate([weighted(pieces, cosines), weighted(pieces, sines)], axis=1)
        spectrum = dot_both(packed, high_ref[residue], low_ref[residue])
        cos_part = spectrum[:, :block]
        sin_part = spectrum[:, block:]
        fc, ic, uc = (cos_part[at * piece : (at + 1) * piece] for at in range(3))
        fs, i_s, us = (sin_part[at * piece : (at + 1) * piece] for at in range(3))
        cc = [fc * ic, fc * uc, uc * ic]
        ss = [fs * i_s, fs * us, us * i_s]
        signs = [-1.0, 1.0, 1.0]
        new_cos = [c + sign * s for c, s, sign in zip(cc, ss, signs)]
        new_sin = [fc * i_s + fs * ic, fc * us - fs * uc, us * ic - uc * i_s]
        new_cos = jnp.concatenate(new_cos, axis=0)
        new_sin = jnp.concatenate(new_sin, axis=0)
        if residue == 0:
            first = lax.broadcasted_iota(jnp.int32, new_cos.shape, 1) == 0
            new_cos = jnp.where(first, 0.5 * jnp.concatenate(cc, axis=0), new_cos)
            new_sin = jnp.where(first, 0.5 * jnp.concatenate(ss, axis=0), new_sin)
        joined = jnp.concatenate([new_cos, new_sin], axis=1) * scale
        back = dot_both(joined, high_ref[residue], low_ref[residue], NT)
        first_half = back[:, :block]
        second_half = back[:, block:]
        for index in range(blocks):
            term = weighted([first_half, second_half], [cosines[index], sines[index]])
            results[index] = term if results[index] is None else results[index] + term
    return results


def greet(devices, count):
    me = lax.axis_index("seq")
    spot = lax.axis_index("red")
    barrier = pltpu.get_barrier_semaphore()
    for step in range(1, devices):
        peer = lax.rem(me + step, devices)
        pl.semaphore_signal(barrier, inc=1, device_id={"seq": peer}, device_id_type=MESH)

    @pl.when(spot > 0)
    def _():
        pl.semaphore_signal(barrier, inc=1, device_id={"red": spot - 1}, device_id_type=MESH)

    @pl.when(spot < count - 1)
    def _():
        pl.semaphore_signal(barrier, inc=1, device_id={"red": spot + 1}, device_id_type=MESH)


def meet(devices, count):
    spot = lax.axis_index("red")
    neighbours = jnp.where(spot > 0, 1, 0) + jnp.where(spot < count - 1, 1, 0)
    pl.semaphore_wait(pltpu.get_barrier_semaphore(), devices - 1 + neighbours)


def exchange(devices, source, target, send_sem, recv_sem, base):
    me = lax.axis_index("seq")
    copies = []
    for step in range(1, devices):
        peer = lax.rem(me + step, devices)
        copy = pltpu.make_async_remote_copy(
            src_ref=source(peer),
            dst_ref=target(me),
            send_sem=send_sem.at[base + step - 1],
            recv_sem=recv_sem.at[base + step - 1],
            device_id={"seq": peer},
            device_id_type=MESH,
        )
        copy.start()
        copies.append(copy)
    return copies


def main_kernel(
    devices, count, chunks, scale_factor,
    tok_ref, emb_ref, wt_ref, filt_ref, cot_ref, high_hbm, low_hbm,
    recv_ref, all_ref,
    part, from_left, from_right, out_sig, sig, sending, one_hot, high_ref, low_ref,
    table_sem, sig_send, sig_recv, res_send, res_recv,
    right_send, right_recv, left_send, left_recv,
    up_send, up_recv, down_send, down_recv,
):
    me = lax.axis_index("seq")
    spot = lax.axis_index("red")
    branches, _, piece, _ = wt_ref.shape
    tok_count, width = filt_ref.shape
    vocabulary = emb_ref.shape[0]
    sub = piece // chunks
    greet(devices, count)
    tables = [
        pltpu.make_async_copy(high_hbm, high_ref, table_sem.at[0]),
        pltpu.make_async_copy(low_hbm, low_ref, table_sem.at[1]),
    ]
    for copy in tables:
        copy.start()
    above_spot = jnp.minimum(spot + 1, count - 1)
    below_spot = jnp.maximum(spot - 1, 0)

    def hop(source, target, slot, sends, recvs, neighbour):
        return pltpu.make_async_remote_copy(
            src_ref=source.at[slot],
            dst_ref=target.at[slot],
            send_sem=sends.at[slot],
            recv_sem=recvs.at[slot],
            device_id={"red": neighbour},
            device_id_type=MESH,
        )

    def right(slot):
        return hop(part, from_left, slot, right_send, right_recv, above_spot)

    def left(slot):
        return hop(part, from_right, slot, left_send, left_recv, below_spot)

    def up(slot):
        return hop(all_ref, all_ref, slot, up_send, up_recv, above_spot)

    def down(slot):
        return hop(all_ref, all_ref, slot, down_send, down_recv, below_spot)

    def products(chunk):
        table = emb_ref[...]
        for group in range(count):
            rows = [wt_ref[b, group, chunk * sub : (chunk + 1) * sub] for b in range(branches)]
            part[chunk * count + group] = dot(jnp.concatenate(rows, axis=0), table, NT)

    def first_hops(chunk):
        base = chunk * count

        @pl.when(spot == 0)
        def _():
            for goal in range(count - 1, 0, -1):
                right(base + goal).start()

        @pl.when(spot == count - 1)
        def _():
            for goal in range(count - 1):
                left(base + goal).start()

    def middle_hops(chunk):
        base = chunk * count
        for tick in range(1, count - 1):
            goal = count - 1 - (tick - spot)

            @pl.when((spot > 0) & (tick >= spot) & (spot < goal))
            def _():
                right(base + goal).wait_recv()
                part[base + goal] = part[base + goal] + from_left[base + goal]
                right(base + goal).start()

            other = tick - (count - 1 - spot)

            @pl.when((spot < count - 1) & (other >= 0) & (spot > other))
            def _():
                left(base + other).wait_recv()
                part[base + other] = part[base + other] + from_right[base + other]
                left(base + other).start()

    def arrive(chunk):
        slot = chunk * count + spot

        @pl.when(spot > 0)
        def _():
            right(slot).wait_recv()
            part[slot] = part[slot] + from_left[slot]

        @pl.when(spot < count - 1)
        def _():
            left(slot).wait_recv()
            part[slot] = part[slot] + from_right[slot]

        return part[slot]

    def share(chunk):
        slot = chunk * count + spot

        @pl.when(spot < count - 1)
        def _():
            up(slot).start()

        @pl.when(spot > 0)
        def _():
            down(slot).start()

    def relay(chunk, step):
        base = chunk * count
        below = spot - step

        @pl.when(below >= 0)
        def _():
            up(base + below).wait_recv()

            @pl.when(spot < count - 1)
            def _():
                up(base + below).start()

        above = spot + step

        @pl.when(above < count)
        def _():
            down(base + above).wait_recv()

            @pl.when(spot > 0)
            def _():
                down(base + above).start()

    def signal_rows(start, rows):
        return jnp.concatenate([sig[at, start : start + rows] for at in range(devices)], axis=1)

    def channels(chunk, own, beside):
        projected = dot_split(own, one_hot[...])
        queries = projected[:sub]
        key_rows = projected[sub : 2 * sub]
        value_rows = projected[2 * sub :]
        filters = signal_rows(chunk * sub, sub)
        cotangent = signal_rows(piece + chunk * sub, sub)
        signals = jnp.concatenate([filters, key_rows * value_rows, cotangent * queries], axis=0)
        results = convolve(signals, high_ref, low_ref, sub, beside)
        rounded = []
        for at in range(devices):
            lanes = slice(at * tok_count, (at + 1) * tok_count)
            conv = results[at][:sub]
            grad_inner = results[at][sub : 2 * sub]
            grads = jnp.concatenate(
                [
                    cotangent[:, lanes] * conv,
                    grad_inner * value_rows[:, lanes],
                    grad_inner * key_rows[:, lanes],
                ],
                axis=0,
            ).astype(jnp.bfloat16)
            rounded.append(grads)
            sending[chunk, at, :sub] = queries[:, lanes] * conv
            sending[chunk, at, sub : 2 * sub] = results[at][2 * sub :] * scale_factor
            sending[chunk, at, 2 * sub :] = grads.astype(jnp.float32)
        all_ref[chunk * count + spot] = dot(jnp.concatenate(rounded, axis=1), one_hot[...], NT)

    filt_t = filt_ref[...].T
    cot_t = cot_ref[...].T
    tok_rows = jnp.broadcast_to(tok_ref[...].astype(jnp.float32), (8, tok_count))
    for peer in range(devices):
        out_sig[peer, :piece] = filt_t[peer * piece : (peer + 1) * piece]
        out_sig[peer, piece : 2 * piece] = cot_t[peer * piece : (peer + 1) * piece]
        out_sig[peer, 2 * piece :] = tok_rows
    products(0)
    meet(devices, count)
    first_hops(0)
    copies = exchange(devices, out_sig.at.__getitem__, sig.at.__getitem__, sig_send, sig_recv, 0)
    for chunk in range(1, chunks):
        products(chunk)
        first_hops(chunk)
    sig[me] = out_sig[me]
    for copy in copies:
        copy.wait_recv()
    ids = signal_rows(2 * piece, 1).astype(jnp.int32)
    vocab_rows = lax.broadcasted_iota(jnp.int32, (vocabulary, devices * tok_count), 0)
    one_hot[...] = jnp.where(vocab_rows == ids, 1.0, 0.0).astype(jnp.bfloat16)
    sent = list(copies)
    arrivals = []
    for chunk in range(chunks):
        middle_hops(chunk)
        if chunk > 0:
            relay(chunk - 1, 1)
        own = arrive(chunk)
        if chunk == 0:
            for copy in tables:
                copy.wait()

        def beside(chunk=chunk):
            if chunk > 0 and count > 2:
                relay(chunk - 1, 2)

        channels(chunk, own, beside)
        share(chunk)
        more = exchange(
            devices,
            lambda peer, chunk=chunk: sending.at[chunk, peer],
            lambda slot, chunk=chunk: recv_ref.at[chunk, slot],
            res_send, res_recv, chunk * (devices - 1),
        )
        recv_ref[chunk, me] = sending[chunk, me]
        sent += more
        arrivals += more
        if chunk > 0:
            for step in range(3, count):
                relay(chunk - 1, step)
    for step in range(1, count):
        relay(chunks - 1, step)
    for chunk in range(chunks):
        base = chunk * count
        for goal in range(count):
            @pl.when(spot < goal)
            def _():
                right(base + goal).wait_send()

            @pl.when(spot > goal)
            def _():
                left(base + goal).wait_send()

        for step in range(count):
            @pl.when((spot - step >= 0) & (spot < count - 1))
            def _():
                up(base + spot - step).wait_send()

            @pl.when((spot + step < count) & (spot > 0))
            def _():
                down(base + spot + step).wait_send()

    for copy in sent:
        copy.wait_send()
    for copy in arrivals:
        copy.wait_recv()


def final_kernel(scale_factor, emb_ref, recv_ref, all_ref, out_ref, filt_ref, grads_ref, weight_ref):
    chunks, devices, rows, _ = recv_ref.shape
    sub = rows // 5
    count = all_ref.shape[0] // chunks
    table = emb_ref[...]
    for chunk in range(chunks):
        for group in range(count):
            product = dot_split(all_ref[chunk * count + group], table) * scale_factor
            for branch in range(3):
                weight_ref[branch, group, chunk * sub : (chunk + 1) * sub] = product[
                    branch * sub : (branch + 1) * sub
                ]

    def positions(at):
        parts = [
            recv_ref[chunk, peer, at * sub : (at + 1) * sub]
            for peer in range(devices)
            for chunk in range(chunks)
        ]
        return jnp.concatenate(parts, axis=0).T

    out_ref[...] = positions(0)
    filt_ref[...] = positions(1)
    for branch in range(3):
        grads_ref[branch] = positions(2 + branch).astype(jnp.bfloat16)


def kernel_shards(devices, count, token_ids, embedding, proj_weight, filters, cotangent):
    tok_count, width = filters.shape
    vocabulary, depth = embedding.shape
    _, branches, _, piece = proj_weight.shape
    scale_factor = float(tok_count * devices) ** (-0.5)
    chunks = CHUNKS
    rows = branches * piece // chunks
    f32 = jnp.float32
    dma = pltpu.SemaphoreType.DMA
    weight_t = jnp.transpose(proj_weight, (1, 2, 3, 0))
    high, low = transform_tables(tok_count, devices)
    block = (chunks * count, rows, vocabulary)
    message = (devices, 2 * piece + 8, tok_count)
    answer = (chunks, devices, 5 * piece // chunks, tok_count)
    received, all_sums = pl.pallas_call(
        functools.partial(main_kernel, devices, count, chunks, scale_factor),
        out_shape=(jax.ShapeDtypeStruct(answer, f32), jax.ShapeDtypeStruct(block, f32)),
        in_specs=[VMEM] * 5 + [pl.BlockSpec(memory_space=pl.ANY)] * 2,
        out_specs=(VMEM, VMEM),
        scratch_shapes=[
            pltpu.VMEM(block, f32),
            pltpu.VMEM(block, f32),
            pltpu.VMEM(block, f32),
            pltpu.VMEM(message, f32),
            pltpu.VMEM(message, f32),
            pltpu.VMEM(answer, f32),
            pltpu.VMEM((vocabulary, devices * tok_count), jnp.bfloat16),
            pltpu.VMEM(high.shape, jnp.bfloat16),
            pltpu.VMEM(low.shape, jnp.bfloat16),
            dma((2,)),
            dma((devices - 1,)),
            dma((devices - 1,)),
            dma((chunks * (devices - 1),)),
            dma((chunks * (devices - 1),)),
        ]
        + [dma((chunks * count,))] * 8,
        compiler_params=pltpu.CompilerParams(collective_id=0, has_side_effects=True),
        name="hyena_exchange",
    )(
        token_ids.reshape(1, tok_count), embedding, weight_t, filters, cotangent,
        jnp.asarray(high), jnp.asarray(low),
    )
    output, filter_grad, grads, weight = pl.pallas_call(
        functools.partial(final_kernel, scale_factor),
        out_shape=(
            jax.ShapeDtypeStruct((tok_count, width), f32),
            jax.ShapeDtypeStruct((tok_count, width), f32),
            jax.ShapeDtypeStruct((branches, tok_count, width), jnp.bfloat16),
            jax.ShapeDtypeStruct((branches, count, piece, depth), f32),
        ),
        in_specs=[VMEM] * 3,
        out_specs=(VMEM,) * 4,
        name="finish",
    )(embedding, received, all_sums)
    return (
        output,
        filter_grad,
        jnp.transpose(grads, (1, 0, 2)),
        jnp.transpose(weight, (3, 0, 1, 2)),
    )


def fits_kernels(devices, count, token_ids, embedding, proj_weight, filters):
    tok_count, width = filters.shape
    vocabulary, depth = embedding.shape
    _, branches, red_count, piece = proj_weight.shape
    lanes = (tok_count, vocabulary, depth)
    aligned = all(size % 128 == 0 for size in lanes) and piece % (16 * CHUNKS) == 0
    tables = devices * (2 * tok_count) ** 2 * 4
    one_hot = vocabulary * tok_count * devices * 8
    held = 4 * branches * piece * vocabulary * (3 * count + 2)
    return (
        aligned
        and branches == 3
        and red_count == count
        and width == devices * piece
        and tables + one_hot + held < 40 * 2**20
    )


def angles(numbers, modulus, direction):
    phase = (numbers % modulus).astype(jnp.float32) * (direction * 2.0 * math.pi / modulus)
    return (jnp.cos(phase), jnp.sin(phase))


def rotate(real_part, imag_part, cosine, sine_part):
    return (real_part * cosine - imag_part * sine_part, real_part * sine_part + imag_part * cosine)


def complex_einsum(formula, matrix, values):
    mat_real, mat_imag = matrix
    val_real, val_imag = values
    real_out = jnp.einsum(formula, mat_real, val_real, precision=precise_mode) - jnp.einsum(
        formula, mat_imag, val_imag, precision=precise_mode
    )
    imag_out = jnp.einsum(formula, mat_real, val_imag, precision=precise_mode) + jnp.einsum(
        formula, mat_imag, val_real, precision=precise_mode
    )
    return (real_out, imag_out)


def factors(length_total):
    first_factor = 1
    for candidate in range(1, math.isqrt(length_total) + 1):
        if length_total % candidate == 0:
            first_factor = candidate
    return (first_factor, length_total // first_factor)


def combine_spectra(spec_real, spec_imag, width):
    filt_re = spec_real[..., :width]
    inner_re = spec_real[..., width : 2 * width]
    up_re = spec_real[..., 2 * width :]
    filt_im = spec_imag[..., :width]
    inner_im = spec_imag[..., width : 2 * width]
    up_im = spec_imag[..., 2 * width :]
    joined_real = jnp.concatenate(
        [
            filt_re * inner_re - filt_im * inner_im,
            filt_re * up_re + filt_im * up_im,
            up_re * inner_re + up_im * inner_im,
        ],
        axis=-1,
    )
    joined_imag = jnp.concatenate(
        [
            filt_re * inner_im + filt_im * inner_re,
            filt_re * up_im - filt_im * up_re,
            up_im * inner_re - up_re * inner_im,
        ],
        axis=-1,
    )
    return (joined_real, joined_imag)


def local_convolve(signals):
    length, branch_count, narrow = signals.shape
    total = 2 * length
    first_factor, second_factor = factors(total)
    flat = signals.reshape(length, branch_count * narrow)
    padded = jnp.concatenate([flat, jnp.zeros_like(flat)], axis=0).reshape(
        first_factor, second_factor, branch_count * narrow
    )
    first_index = jnp.arange(first_factor, dtype=jnp.int32)
    second_index = jnp.arange(second_factor, dtype=jnp.int32)
    cosine, sine_part = angles(first_index[:, None] * first_index[None, :], first_factor, -1.0)
    real_part = jnp.einsum("kn,nbm->kbm", cosine, padded, precision=precise_mode)
    imag_part = jnp.einsum("kn,nbm->kbm", sine_part, padded, precision=precise_mode)
    cosine, sine_part = angles(first_index[:, None] * second_index[None, :], total, -1.0)
    real_part, imag_part = rotate(real_part, imag_part, cosine[:, :, None], sine_part[:, :, None])
    real_part, imag_part = complex_einsum(
        "lb,kbm->klm",
        angles(second_index[:, None] * second_index[None, :], second_factor, -1.0),
        (real_part, imag_part),
    )
    real_part, imag_part = combine_spectra(real_part, imag_part, narrow)
    real_part, imag_part = complex_einsum(
        "bl,klm->kbm",
        angles(second_index[:, None] * second_index[None, :], second_factor, 1.0),
        (real_part, imag_part),
    )
    cosine, sine_part = angles(first_index[:, None] * second_index[None, :], total, 1.0)
    real_part, imag_part = rotate(real_part, imag_part, cosine[:, :, None], sine_part[:, :, None])
    cosine, sine_part = angles(first_index[:, None] * first_index[None, :], first_factor, 1.0)
    result = jnp.einsum("nk,kbm->nbm", cosine, real_part, precision=precise_mode) - jnp.einsum(
        "nk,kbm->nbm", sine_part, imag_part, precision=precise_mode
    )
    result = result.reshape(total, branch_count * narrow)[:length] / total
    return result.reshape(length, branch_count, narrow)


def shards(token_ids, embedding, proj_weight, filters, cotangent):
    tok_count = token_ids.shape[0]
    devices = lax.axis_size("seq")
    count = lax.axis_size("red")
    if fits_kernels(devices, count, token_ids, embedding, proj_weight, filters):
        return kernel_shards(
            devices, count, token_ids, embedding, proj_weight, filters, cotangent
        )
    width = filters.shape[1]
    vocabulary = embedding.shape[0]
    width_rows, branches, red_count, piece = proj_weight.shape
    scale_factor = float(tok_count * devices) ** (-0.5)
    table = jnp.dot(
        embedding,
        proj_weight.reshape(width_rows, branches * red_count * piece),
        preferred_element_type=jnp.float32,
    )
    table = table.reshape(vocabulary, branches, red_count, piece)
    own_table = lax.psum_scatter(table, "red", scatter_dimension=2, tiled=True)
    full_table = lax.all_gather(own_table, "seq", axis=3, tiled=True)
    projected = jnp.take(full_table, token_ids, axis=0)
    projected = projected.reshape(tok_count, branches, width)
    queries = projected[:, 0]
    key_rows = projected[:, 1]
    value_rows = projected[:, 2]
    inner = key_rows * value_rows
    upstream = cotangent * queries
    stacked = jnp.stack([filters, inner, upstream], axis=1)
    whole_length = lax.all_to_all(stacked, "seq", split_axis=2, concat_axis=0, tiled=True)
    results = local_convolve(whole_length)
    returned = lax.all_to_all(results, "seq", split_axis=0, concat_axis=2, tiled=True)
    conv = returned[:, 0]
    grad_inner = returned[:, 1]
    filter_raw = returned[:, 2]
    output = queries * conv
    filter_grad = filter_raw * scale_factor
    branch_grads = jnp.stack(
        [cotangent * conv, grad_inner * value_rows, grad_inner * key_rows], axis=1
    ).astype(jnp.bfloat16)
    one_hot = (token_ids[:, None] == lax.iota(jnp.int32, vocabulary)[None, :]).astype(jnp.bfloat16)
    token_sums = lax.dot_general(
        one_hot,
        branch_grads.reshape(tok_count, branches * width),
        (((0,), (0,)), ((), ())),
        preferred_element_type=jnp.float32,
    )
    summed = lax.psum_scatter(
        token_sums.reshape(vocabulary, branches, width), "seq", scatter_dimension=2, tiled=True
    )
    gathered = lax.all_gather(summed[:, :, None, :], "red", axis=2, tiled=True)
    weight_grad = (
        lax.dot_general(
            embedding.astype(jnp.float32),
            gathered.reshape(vocabulary, branches * red_count * piece),
            (((0,), (0,)), ((), ())),
            precision=precise_mode,
        )
        * scale_factor
    )
    return (
        output,
        filter_grad,
        branch_grads,
        weight_grad.reshape(width_rows, branches, red_count, piece),
    )


def solution(mesh):
    in_specs = (
        P("seq"),
        P(None, "red"),
        P("red", None, None, "seq"),
        P("seq", "red"),
        P("seq", "red"),
    )
    out_specs = (
        P("seq", "red"),
        P("seq", "red"),
        P("seq", None, "red"),
        P("red", None, None, "seq"),
    )
    return jax.shard_map(shards, mesh=mesh, in_specs=in_specs, out_specs=out_specs, check_vma=False)
```

```python
import functools
import math

import jax
import jax.numpy as jnp
import numpy as np
from jax import lax
from jax.experimental import pallas as pl
from jax.experimental.pallas import tpu as pltpu
from jax.sharding import PartitionSpec as P

precise_mode = lax.Precision.HIGHEST
MESH = pl.DeviceIdType.MESH
VMEM = pl.BlockSpec(memory_space=pltpu.VMEM)
CHUNKS = 1
NN = (((1,), (0,)), ((), ()))
NT = (((1,), (1,)), ((), ()))


def split(value):
    high = value.astype(jnp.bfloat16)
    low = (value - high.astype(jnp.float32)).astype(jnp.bfloat16)
    return high, low


def dot(left, right, dims=NN):
    return lax.dot_general(left, right, dims, preferred_element_type=jnp.float32)


def dot_split(value, matrix, dims=NN):
    high, low = split(value)
    both = dot(jnp.concatenate([high, low], axis=0), matrix, dims)
    rows = value.shape[0]
    return both[:rows] + both[rows:]


def dot_both(value, matrix_high, matrix_low, dims=NN):
    high, _ = split(value)
    return dot_split(value, matrix_high, dims) + dot(high, matrix_low, dims)


def transform_tables(block, blocks):
    total = 2 * blocks * block
    place = np.arange(block)
    half = block // 2
    tables = np.zeros((blocks, 2 * block, 2 * block))
    even = 2 * np.pi * ((2 * blocks * place[:, None] * np.arange(half)[None, :]) % total) / total
    odd = 2 * np.pi * ((place[:, None] * (blocks + 2 * blocks * np.arange(half))[None, :]) % total) / total
    tables[0, :block, :half] = np.cos(even)
    tables[0, :block, block : block + half] = np.sin(even)
    tables[0, :block, block] = 1.0 - 2.0 * (place % 2)
    tables[0, block:, half:block] = np.cos(odd)
    tables[0, block:, block + half :] = np.sin(odd)
    for residue in range(1, blocks):
        freq = residue + 2 * blocks * np.arange(block)
        psi = 2 * np.pi * ((place[:, None] * freq[None, :]) % total) / total
        tables[residue, :block, :block] = np.cos(psi)
        tables[residue, :block, block:] = np.sin(psi)
        tables[residue, block:, :block] = -np.sin(psi)
        tables[residue, block:, block:] = np.cos(psi)
    tables = tables.astype(np.float32)
    high = tables.astype(jnp.bfloat16)
    low = (tables - high.astype(np.float32)).astype(jnp.bfloat16)
    return high, low


def phases(residue, blocks):
    if residue == 0:
        return [1.0] * blocks, [(-1.0) ** index for index in range(blocks)]
    turn = [math.pi * ((residue * index) % (2 * blocks)) / blocks for index in range(blocks)]
    return [math.cos(a) for a in turn], [math.sin(a) for a in turn]


def weighted(terms, weights):
    total = None
    for term, weight in zip(terms, weights):
        if abs(weight) < 1e-12:
            continue
        part = term if weight == 1.0 else term * weight
        total = part if total is None else total + part
    return total


def convolve(signals, high_ref, low_ref, piece, beside):
    blocks, double, _ = high_ref.shape
    block = double // 2
    pieces = [signals[:, index * block : (index + 1) * block] for index in range(blocks)]
    results = [None] * blocks
    scale = 1.0 / (blocks * block)
    for residue in range(blocks):
        if residue == blocks // 2:
            beside()
        cosines, sines = phases(residue, blocks)
        packed = jnp.concatenate([weighted(pieces, cosines), weighted(pieces, sines)], axis=1)
        spectrum = dot_both(packed, high_ref[residue], low_ref[residue])
        cos_part = spectrum[:, :block]
        sin_part = spectrum[:, block:]
        fc, ic, uc = (cos_part[at * piece : (at + 1) * piece] for at in range(3))
        fs, i_s, us = (sin_part[at * piece : (at + 1) * piece] for at in range(3))
        cc = [fc * ic, fc * uc, uc * ic]
        ss = [fs * i_s, fs * us, us * i_s]
        signs = [-1.0, 1.0, 1.0]
        new_cos = [c + sign * s for c, s, sign in zip(cc, ss, signs)]
        new_sin = [fc * i_s + fs * ic, fc * us - fs * uc, us * ic - uc * i_s]
        new_cos = jnp.concatenate(new_cos, axis=0)
        new_sin = jnp.concatenate(new_sin, axis=0)
        if residue == 0:
            first = lax.broadcasted_iota(jnp.int32, new_cos.shape, 1) == 0
            new_cos = jnp.where(first, 0.5 * jnp.concatenate(cc, axis=0), new_cos)
            new_sin = jnp.where(first, 0.5 * jnp.concatenate(ss, axis=0), new_sin)
        joined = jnp.concatenate([new_cos, new_sin], axis=1) * scale
        back = dot_both(joined, high_ref[residue], low_ref[residue], NT)
        first_half = back[:, :block]
        second_half = back[:, block:]
        for index in range(blocks):
            term = weighted([first_half, second_half], [cosines[index], sines[index]])
            results[index] = term if results[index] is None else results[index] + term
    return results


def greet(devices, count):
    me = lax.axis_index("seq")
    spot = lax.axis_index("red")
    barrier = pltpu.get_barrier_semaphore()
    for step in range(1, devices):
        peer = lax.rem(me + step, devices)
        pl.semaphore_signal(barrier, inc=1, device_id={"seq": peer}, device_id_type=MESH)

    @pl.when(spot > 0)
    def _():
        pl.semaphore_signal(barrier, inc=1, device_id={"red": spot - 1}, device_id_type=MESH)

    @pl.when(spot < count - 1)
    def _():
        pl.semaphore_signal(barrier, inc=1, device_id={"red": spot + 1}, device_id_type=MESH)


def meet(devices, count):
    spot = lax.axis_index("red")
    neighbours = jnp.where(spot > 0, 1, 0) + jnp.where(spot < count - 1, 1, 0)
    pl.semaphore_wait(pltpu.get_barrier_semaphore(), devices - 1 + neighbours)


def exchange(devices, source, target, send_sem, recv_sem, base):
    me = lax.axis_index("seq")
    copies = []
    for step in range(1, devices):
        peer = lax.rem(me + step, devices)
        copy = pltpu.make_async_remote_copy(
            src_ref=source(peer),
            dst_ref=target(me),
            send_sem=send_sem.at[base + step - 1],
            recv_sem=recv_sem.at[base + step - 1],
            device_id={"seq": peer},
            device_id_type=MESH,
        )
        copy.start()
        copies.append(copy)
    return copies


def main_kernel(
    devices, count, chunks, scale_factor,
    tok_ref, emb_ref, wt_ref, filt_ref, cot_ref, high_hbm, low_hbm,
    recv_ref, all_ref,
    part, from_left, from_right, out_sig, sig, sending, one_hot, high_ref, low_ref,
    table_sem, sig_send, sig_recv, res_send, res_recv,
    right_send, right_recv, left_send, left_recv,
    up_send, up_recv, down_send, down_recv,
):
    me = lax.axis_index("seq")
    spot = lax.axis_index("red")
    branches, _, piece, _ = wt_ref.shape
    tok_count, width = filt_ref.shape
    vocabulary = emb_ref.shape[0]
    sub = piece // chunks
    greet(devices, count)
    tables = [
        pltpu.make_async_copy(high_hbm, high_ref, table_sem.at[0]),
        pltpu.make_async_copy(low_hbm, low_ref, table_sem.at[1]),
    ]
    for copy in tables:
        copy.start()
    above_spot = jnp.minimum(spot + 1, count - 1)
    below_spot = jnp.maximum(spot - 1, 0)

    def hop(source, target, slot, sends, recvs, neighbour):
        return pltpu.make_async_remote_copy(
            src_ref=source.at[slot],
            dst_ref=target.at[slot],
            send_sem=sends.at[slot],
            recv_sem=recvs.at[slot],
            device_id={"red": neighbour},
            device_id_type=MESH,
        )

    def right(slot):
        return hop(part, from_left, slot, right_send, right_recv, above_spot)

    def left(slot):
        return hop(part, from_right, slot, left_send, left_recv, below_spot)

    def up(slot):
        return hop(all_ref, all_ref, slot, up_send, up_recv, above_spot)

    def down(slot):
        return hop(all_ref, all_ref, slot, down_send, down_recv, below_spot)

    def products(chunk):
        table = emb_ref[...]
        for group in range(count):
            rows = [wt_ref[b, group, chunk * sub : (chunk + 1) * sub] for b in range(branches)]
            part[chunk * count + group] = dot(jnp.concatenate(rows, axis=0), table, NT)

    def first_hops(chunk):
        base = chunk * count

        @pl.when(spot == 0)
        def _():
            for goal in range(count - 1, 0, -1):
                right(base + goal).start()

        @pl.when(spot == count - 1)
        def _():
            for goal in range(count - 1):
                left(base + goal).start()

    def middle_hops(chunk):
        base = chunk * count
        for tick in range(1, count - 1):
            goal = count - 1 - (tick - spot)

            @pl.when((spot > 0) & (tick >= spot) & (spot < goal))
            def _():
                right(base + goal).wait_recv()
                part[base + goal] = part[base + goal] + from_left[base + goal]
                right(base + goal).start()

            other = tick - (count - 1 - spot)

            @pl.when((spot < count - 1) & (other >= 0) & (spot > other))
            def _():
                left(base + other).wait_recv()
                part[base + other] = part[base + other] + from_right[base + other]
                left(base + other).start()

    def arrive(chunk):
        slot = chunk * count + spot

        @pl.when(spot > 0)
        def _():
            right(slot).wait_recv()
            part[slot] = part[slot] + from_left[slot]

        @pl.when(spot < count - 1)
        def _():
            left(slot).wait_recv()
            part[slot] = part[slot] + from_right[slot]

        return part[slot]

    def share(chunk):
        slot = chunk * count + spot

        @pl.when(spot < count - 1)
        def _():
            up(slot).start()

        @pl.when(spot > 0)
        def _():
            down(slot).start()

    def relay(chunk, step):
        base = chunk * count
        below = spot - step

        @pl.when(below >= 0)
        def _():
            up(base + below).wait_recv()

            @pl.when(spot < count - 1)
            def _():
                up(base + below).start()

        above = spot + step

        @pl.when(above < count)
        def _():
            down(base + above).wait_recv()

            @pl.when(spot > 0)
            def _():
                down(base + above).start()

    def signal_rows(start, rows):
        return jnp.concatenate([sig[at, start : start + rows] for at in range(devices)], axis=1)

    def channels(chunk, own, beside):
        projected = dot_split(own, one_hot[...])
        queries = projected[:sub]
        key_rows = projected[sub : 2 * sub]
        value_rows = projected[2 * sub :]
        filters = signal_rows(chunk * sub, sub)
        cotangent = signal_rows(piece + chunk * sub, sub)
        signals = jnp.concatenate([filters, key_rows * value_rows, cotangent * queries], axis=0)
        results = convolve(signals, high_ref, low_ref, sub, beside)
        rounded = []
        for at in range(devices):
            lanes = slice(at * tok_count, (at + 1) * tok_count)
            conv = results[at][:sub]
            grad_inner = results[at][sub : 2 * sub]
            grads = jnp.concatenate(
                [
                    cotangent[:, lanes] * conv,
                    grad_inner * value_rows[:, lanes],
                    grad_inner * key_rows[:, lanes],
                ],
                axis=0,
            ).astype(jnp.bfloat16)
            rounded.append(grads)
            sending[chunk, at, :sub] = queries[:, lanes] * conv
            sending[chunk, at, sub : 2 * sub] = results[at][2 * sub :] * scale_factor
            sending[chunk, at, 2 * sub :] = grads.astype(jnp.float32)
        all_ref[chunk * count + spot] = dot(jnp.concatenate(rounded, axis=1), one_hot[...], NT)

    filt_t = filt_ref[...].T
    cot_t = cot_ref[...].T
    tok_rows = jnp.broadcast_to(tok_ref[...].astype(jnp.float32), (8, tok_count))
    for peer in range(devices):
        out_sig[peer, :piece] = filt_t[peer * piece : (peer + 1) * piece]
        out_sig[peer, piece : 2 * piece] = cot_t[peer * piece : (peer + 1) * piece]
        out_sig[peer, 2 * piece :] = tok_rows
    products(0)
    meet(devices, count)
    first_hops(0)
    copies = exchange(devices, out_sig.at.__getitem__, sig.at.__getitem__, sig_send, sig_recv, 0)
    for chunk in range(1, chunks):
        products(chunk)
        first_hops(chunk)
    sig[me] = out_sig[me]
    for copy in copies:
        copy.wait_recv()
    ids = signal_rows(2 * piece, 1).astype(jnp.int32)
    vocab_rows = lax.broadcasted_iota(jnp.int32, (vocabulary, devices * tok_count), 0)
    one_hot[...] = jnp.where(vocab_rows == ids, 1.0, 0.0).astype(jnp.bfloat16)
    sent = list(copies)
    arrivals = []
    for chunk in range(chunks):
        middle_hops(chunk)
        if chunk > 0:
            relay(chunk - 1, 1)
        own = arrive(chunk)
        if chunk == 0:
            for copy in tables:
                copy.wait()

        def beside(chunk=chunk):
            if chunk > 0 and count > 2:
                relay(chunk - 1, 2)

        channels(chunk, own, beside)
        share(chunk)
        more = exchange(
            devices,
            lambda peer, chunk=chunk: sending.at[chunk, peer],
            lambda slot, chunk=chunk: recv_ref.at[chunk, slot],
            res_send, res_recv, chunk * (devices - 1),
        )
        recv_ref[chunk, me] = sending[chunk, me]
        sent += more
        arrivals += more
        if chunk > 0:
            for step in range(3, count):
                relay(chunk - 1, step)
    for step in range(1, count):
        relay(chunks - 1, step)
    for chunk in range(chunks):
        base = chunk * count
        for goal in range(count):
            @pl.when(spot < goal)
            def _():
                right(base + goal).wait_send()

            @pl.when(spot > goal)
            def _():
                left(base + goal).wait_send()

        for step in range(count):
            @pl.when((spot - step >= 0) & (spot < count - 1))
            def _():
                up(base + spot - step).wait_send()

            @pl.when((spot + step < count) & (spot > 0))
            def _():
                down(base + spot + step).wait_send()

    for copy in sent:
        copy.wait_send()
    for copy in arrivals:
        copy.wait_recv()


def final_kernel(scale_factor, emb_ref, recv_ref, all_ref, out_ref, filt_ref, grads_ref, weight_ref):
    chunks, devices, rows, _ = recv_ref.shape
    sub = rows // 5
    count = all_ref.shape[0] // chunks
    table = emb_ref[...]
    for chunk in range(chunks):
        for group in range(count):
            product = dot_split(all_ref[chunk * count + group], table) * scale_factor
            for branch in range(3):
                weight_ref[branch, group, chunk * sub : (chunk + 1) * sub] = product[
                    branch * sub : (branch + 1) * sub
                ]

    def positions(at):
        parts = [
            recv_ref[chunk, peer, at * sub : (at + 1) * sub]
            for peer in range(devices)
            for chunk in range(chunks)
        ]
        return jnp.concatenate(parts, axis=0).T

    out_ref[...] = positions(0)
    filt_ref[...] = positions(1)
    for branch in range(3):
        grads_ref[branch] = positions(2 + branch).astype(jnp.bfloat16)


def kernel_shards(devices, count, token_ids, embedding, proj_weight, filters, cotangent):
    tok_count, width = filters.shape
    vocabulary, depth = embedding.shape
    _, branches, _, piece = proj_weight.shape
    scale_factor = float(tok_count * devices) ** (-0.5)
    chunks = CHUNKS
    rows = branches * piece // chunks
    f32 = jnp.float32
    dma = pltpu.SemaphoreType.DMA
    weight_t = jnp.transpose(proj_weight, (1, 2, 3, 0))
    high, low = transform_tables(tok_count, devices)
    block = (chunks * count, rows, vocabulary)
    message = (devices, 2 * piece + 8, tok_count)
    answer = (chunks, devices, 5 * piece // chunks, tok_count)
    received, all_sums = pl.pallas_call(
        functools.partial(main_kernel, devices, count, chunks, scale_factor),
        out_shape=(jax.ShapeDtypeStruct(answer, f32), jax.ShapeDtypeStruct(block, f32)),
        in_specs=[VMEM] * 5 + [pl.BlockSpec(memory_space=pl.ANY)] * 2,
        out_specs=(VMEM, VMEM),
        scratch_shapes=[
            pltpu.VMEM(block, f32),
            pltpu.VMEM(block, f32),
            pltpu.VMEM(block, f32),
            pltpu.VMEM(message, f32),
            pltpu.VMEM(message, f32),
            pltpu.VMEM(answer, f32),
            pltpu.VMEM((vocabulary, devices * tok_count), jnp.bfloat16),
            pltpu.VMEM(high.shape, jnp.bfloat16),
            pltpu.VMEM(low.shape, jnp.bfloat16),
            dma((2,)),
            dma((devices - 1,)),
            dma((devices - 1,)),
            dma((chunks * (devices - 1),)),
            dma((chunks * (devices - 1),)),
        ]
        + [dma((chunks * count,))] * 8,
        compiler_params=pltpu.CompilerParams(collective_id=0, has_side_effects=True),
        name="hyena_exchange",
    )(
        token_ids.reshape(1, tok_count), embedding, weight_t, filters, cotangent,
        jnp.asarray(high), jnp.asarray(low),
    )
    output, filter_grad, grads, weight = pl.pallas_call(
        functools.partial(final_kernel, scale_factor),
        out_shape=(
            jax.ShapeDtypeStruct((tok_count, width), f32),
            jax.ShapeDtypeStruct((tok_count, width), f32),
            jax.ShapeDtypeStruct((branches, tok_count, width), jnp.bfloat16),
            jax.ShapeDtypeStruct((branches, count, piece, depth), f32),
        ),
        in_specs=[VMEM] * 3,
        out_specs=(VMEM,) * 4,
        name="finish",
    )(embedding, received, all_sums)
    return (
        output,
        filter_grad,
        jnp.transpose(grads, (1, 0, 2)),
        jnp.transpose(weight, (3, 0, 1, 2)),
    )


def fits_kernels(devices, count, token_ids, embedding, proj_weight, filters):
    tok_count, width = filters.shape
    vocabulary, depth = embedding.shape
    _, branches, red_count, piece = proj_weight.shape
    lanes = (tok_count, vocabulary, depth)
    aligned = all(size % 128 == 0 for size in lanes) and piece % (16 * CHUNKS) == 0
    tables = devices * (2 * tok_count) ** 2 * 4
    one_hot = vocabulary * tok_count * devices * 8
    held = 4 * branches * piece * vocabulary * (3 * count + 2)
    return (
        aligned
        and branches == 3
        and red_count == count
        and width == devices * piece
        and tables + one_hot + held < 40 * 2**20
    )


def angles(numbers, modulus, direction):
    phase = (numbers % modulus).astype(jnp.float32) * (direction * 2.0 * math.pi / modulus)
    return (jnp.cos(phase), jnp.sin(phase))


def rotate(real_part, imag_part, cosine, sine_part):
    return (real_part * cosine - imag_part * sine_part, real_part * sine_part + imag_part * cosine)


def complex_einsum(formula, matrix, values):
    mat_real, mat_imag = matrix
    val_real, val_imag = values
    real_out = jnp.einsum(formula, mat_real, val_real, precision=precise_mode) - jnp.einsum(
        formula, mat_imag, val_imag, precision=precise_mode
    )
    imag_out = jnp.einsum(formula, mat_real, val_imag, precision=precise_mode) + jnp.einsum(
        formula, mat_imag, val_real, precision=precise_mode
    )
    return (real_out, imag_out)


def factors(length_total):
    first_factor = 1
    for candidate in range(1, math.isqrt(length_total) + 1):
        if length_total % candidate == 0:
            first_factor = candidate
    return (first_factor, length_total // first_factor)


def combine_spectra(spec_real, spec_imag, width):
    filt_re = spec_real[..., :width]
    inner_re = spec_real[..., width : 2 * width]
    up_re = spec_real[..., 2 * width :]
    filt_im = spec_imag[..., :width]
    inner_im = spec_imag[..., width : 2 * width]
    up_im = spec_imag[..., 2 * width :]
    joined_real = jnp.concatenate(
        [
            filt_re * inner_re - filt_im * inner_im,
            filt_re * up_re + filt_im * up_im,
            up_re * inner_re + up_im * inner_im,
        ],
        axis=-1,
    )
    joined_imag = jnp.concatenate(
        [
            filt_re * inner_im + filt_im * inner_re,
            filt_re * up_im - filt_im * up_re,
            up_im * inner_re - up_re * inner_im,
        ],
        axis=-1,
    )
    return (joined_real, joined_imag)


def local_convolve(signals):
    length, branch_count, narrow = signals.shape
    total = 2 * length
    first_factor, second_factor = factors(total)
    flat = signals.reshape(length, branch_count * narrow)
    padded = jnp.concatenate([flat, jnp.zeros_like(flat)], axis=0).reshape(
        first_factor, second_factor, branch_count * narrow
    )
    first_index = jnp.arange(first_factor, dtype=jnp.int32)
    second_index = jnp.arange(second_factor, dtype=jnp.int32)
    cosine, sine_part = angles(first_index[:, None] * first_index[None, :], first_factor, -1.0)
    real_part = jnp.einsum("kn,nbm->kbm", cosine, padded, precision=precise_mode)
    imag_part = jnp.einsum("kn,nbm->kbm", sine_part, padded, precision=precise_mode)
    cosine, sine_part = angles(first_index[:, None] * second_index[None, :], total, -1.0)
    real_part, imag_part = rotate(real_part, imag_part, cosine[:, :, None], sine_part[:, :, None])
    real_part, imag_part = complex_einsum(
        "lb,kbm->klm",
        angles(second_index[:, None] * second_index[None, :], second_factor, -1.0),
        (real_part, imag_part),
    )
    real_part, imag_part = combine_spectra(real_part, imag_part, narrow)
    real_part, imag_part = complex_einsum(
        "bl,klm->kbm",
        angles(second_index[:, None] * second_index[None, :], second_factor, 1.0),
        (real_part, imag_part),
    )
    cosine, sine_part = angles(first_index[:, None] * second_index[None, :], total, 1.0)
    real_part, imag_part = rotate(real_part, imag_part, cosine[:, :, None], sine_part[:, :, None])
    cosine, sine_part = angles(first_index[:, None] * first_index[None, :], first_factor, 1.0)
    result = jnp.einsum("nk,kbm->nbm", cosine, real_part, precision=precise_mode) - jnp.einsum(
        "nk,kbm->nbm", sine_part, imag_part, precision=precise_mode
    )
    result = result.reshape(total, branch_count * narrow)[:length] / total
    return result.reshape(length, branch_count, narrow)


def shards(token_ids, embedding, proj_weight, filters, cotangent):
    tok_count = token_ids.shape[0]
    devices = lax.axis_size("seq")
    count = lax.axis_size("red")
    if fits_kernels(devices, count, token_ids, embedding, proj_weight, filters):
        return kernel_shards(
            devices, count, token_ids, embedding, proj_weight, filters, cotangent
        )
    width = filters.shape[1]
    vocabulary = embedding.shape[0]
    width_rows, branches, red_count, piece = proj_weight.shape
    scale_factor = float(tok_count * devices) ** (-0.5)
    table = jnp.dot(
        embedding,
        proj_weight.reshape(width_rows, branches * red_count * piece),
        preferred_element_type=jnp.float32,
    )
    table = table.reshape(vocabulary, branches, red_count, piece)
    own_table = lax.psum_scatter(table, "red", scatter_dimension=2, tiled=True)
    full_table = lax.all_gather(own_table, "seq", axis=3, tiled=True)
    projected = jnp.take(full_table, token_ids, axis=0)
    projected = projected.reshape(tok_count, branches, width)
    queries = projected[:, 0]
    key_rows = projected[:, 1]
    value_rows = projected[:, 2]
    inner = key_rows * value_rows
    upstream = cotangent * queries
    stacked = jnp.stack([filters, inner, upstream], axis=1)
    whole_length = lax.all_to_all(stacked, "seq", split_axis=2, concat_axis=0, tiled=True)
    results = local_convolve(whole_length)
    returned = lax.all_to_all(results, "seq", split_axis=0, concat_axis=2, tiled=True)
    conv = returned[:, 0]
    grad_inner = returned[:, 1]
    filter_raw = returned[:, 2]
    output = queries * conv
    filter_grad = filter_raw * scale_factor
    branch_grads = jnp.stack(
        [cotangent * conv, grad_inner * value_rows, grad_inner * key_rows], axis=1
    ).astype(jnp.bfloat16)
    one_hot = (token_ids[:, None] == lax.iota(jnp.int32, vocabulary)[None, :]).astype(jnp.bfloat16)
    token_sums = lax.dot_general(
        one_hot,
        branch_grads.reshape(tok_count, branches * width),
        (((0,), (0,)), ((), ())),
        preferred_element_type=jnp.float32,
    )
    summed = lax.psum_scatter(
        token_sums.reshape(vocabulary, branches, width), "seq", scatter_dimension=2, tiled=True
    )
    gathered = lax.all_gather(summed[:, :, None, :], "red", axis=2, tiled=True)
    weight_grad = (
        lax.dot_general(
            embedding.astype(jnp.float32),
            gathered.reshape(vocabulary, branches * red_count * piece),
            (((0,), (0,)), ((), ())),
            precision=precise_mode,
        )
        * scale_factor
    )
    return (
        output,
        filter_grad,
        branch_grads,
        weight_grad.reshape(width_rows, branches, red_count, piece),
    )


def solution(mesh):
    in_specs = (
        P("seq"),
        P(None, "red"),
        P("red", None, None, "seq"),
        P("seq", "red"),
        P("seq", "red"),
    )
    out_specs = (
        P("seq", "red"),
        P("seq", "red"),
        P("seq", None, "red"),
        P("red", None, None, "seq"),
    )
    return jax.shard_map(shards, mesh=mesh, in_specs=in_specs, out_specs=out_specs, check_vma=False)
```

```python
import functools
import math

import jax
import jax.numpy as jnp
import numpy as np
from jax import lax
from jax.experimental import pallas as pl
from jax.experimental.pallas import tpu as pltpu
from jax.sharding import PartitionSpec as P

precise_mode = lax.Precision.HIGHEST
MESH = pl.DeviceIdType.MESH
VMEM = pl.BlockSpec(memory_space=pltpu.VMEM)
CHUNKS = 1
NN = (((1,), (0,)), ((), ()))
NT = (((1,), (1,)), ((), ()))


def split(value):
    high = value.astype(jnp.bfloat16)
    low = (value - high.astype(jnp.float32)).astype(jnp.bfloat16)
    return high, low


def dot(left, right, dims=NN):
    return lax.dot_general(left, right, dims, preferred_element_type=jnp.float32)


def dot_split(value, matrix, dims=NN):
    high, low = split(value)
    both = dot(jnp.concatenate([high, low], axis=0), matrix, dims)
    rows = value.shape[0]
    return both[:rows] + both[rows:]


def dot_both(value, matrix_high, matrix_low, dims=NN):
    high, _ = split(value)
    return dot_split(value, matrix_high, dims) + dot(high, matrix_low, dims)


def transform_tables(block, blocks):
    total = 2 * blocks * block
    place = np.arange(block)
    half = block // 2
    tables = np.zeros((blocks, 2 * block, 2 * block))
    even = 2 * np.pi * ((2 * blocks * place[:, None] * np.arange(half)[None, :]) % total) / total
    odd = 2 * np.pi * ((place[:, None] * (blocks + 2 * blocks * np.arange(half))[None, :]) % total) / total
    tables[0, :block, :half] = np.cos(even)
    tables[0, :block, block : block + half] = np.sin(even)
    tables[0, :block, block] = 1.0 - 2.0 * (place % 2)
    tables[0, block:, half:block] = np.cos(odd)
    tables[0, block:, block + half :] = np.sin(odd)
    for residue in range(1, blocks):
        freq = residue + 2 * blocks * np.arange(block)
        psi = 2 * np.pi * ((place[:, None] * freq[None, :]) % total) / total
        tables[residue, :block, :block] = np.cos(psi)
        tables[residue, :block, block:] = np.sin(psi)
        tables[residue, block:, :block] = -np.sin(psi)
        tables[residue, block:, block:] = np.cos(psi)
    tables = tables.astype(np.float32)
    high = tables.astype(jnp.bfloat16)
    low = (tables - high.astype(np.float32)).astype(jnp.bfloat16)
    return high, low


def phases(residue, blocks):
    if residue == 0:
        return [1.0] * blocks, [(-1.0) ** index for index in range(blocks)]
    turn = [math.pi * ((residue * index) % (2 * blocks)) / blocks for index in range(blocks)]
    return [math.cos(a) for a in turn], [math.sin(a) for a in turn]


def weighted(terms, weights):
    total = None
    for term, weight in zip(terms, weights):
        if abs(weight) < 1e-12:
            continue
        part = term if weight == 1.0 else term * weight
        total = part if total is None else total + part
    return total


def convolve(signals, high_ref, low_ref, piece, beside):
    blocks, double, _ = high_ref.shape
    block = double // 2
    pieces = [signals[:, index * block : (index + 1) * block] for index in range(blocks)]
    results = [None] * blocks
    scale = 1.0 / (blocks * block)
    for residue in range(blocks):
        if residue == blocks // 2:
            beside()
        cosines, sines = phases(residue, blocks)
        packed = jnp.concatenate([weighted(pieces, cosines), weighted(pieces, sines)], axis=1)
        spectrum = dot_both(packed, high_ref[residue], low_ref[residue])
        cos_part = spectrum[:, :block]
        sin_part = spectrum[:, block:]
        fc, ic, uc = (cos_part[at * piece : (at + 1) * piece] for at in range(3))
        fs, i_s, us = (sin_part[at * piece : (at + 1) * piece] for at in range(3))
        cc = [fc * ic, fc * uc, uc * ic]
        ss = [fs * i_s, fs * us, us * i_s]
        signs = [-1.0, 1.0, 1.0]
        new_cos = [c + sign * s for c, s, sign in zip(cc, ss, signs)]
        new_sin = [fc * i_s + fs * ic, fc * us - fs * uc, us * ic - uc * i_s]
        new_cos = jnp.concatenate(new_cos, axis=0)
        new_sin = jnp.concatenate(new_sin, axis=0)
        if residue == 0:
            first = lax.broadcasted_iota(jnp.int32, new_cos.shape, 1) == 0
            new_cos = jnp.where(first, 0.5 * jnp.concatenate(cc, axis=0), new_cos)
            new_sin = jnp.where(first, 0.5 * jnp.concatenate(ss, axis=0), new_sin)
        joined = jnp.concatenate([new_cos, new_sin], axis=1) * scale
        back = dot_both(joined, high_ref[residue], low_ref[residue], NT)
        first_half = back[:, :block]
        second_half = back[:, block:]
        for index in range(blocks):
            term = weighted([first_half, second_half], [cosines[index], sines[index]])
            results[index] = term if results[index] is None else results[index] + term
    return results


def greet(devices, count):
    me = lax.axis_index("seq")
    spot = lax.axis_index("red")
    barrier = pltpu.get_barrier_semaphore()
    for step in range(1, devices):
        peer = lax.rem(me + step, devices)
        pl.semaphore_signal(barrier, inc=1, device_id={"seq": peer}, device_id_type=MESH)

    @pl.when(spot > 0)
    def _():
        pl.semaphore_signal(barrier, inc=1, device_id={"red": spot - 1}, device_id_type=MESH)

    @pl.when(spot < count - 1)
    def _():
        pl.semaphore_signal(barrier, inc=1, device_id={"red": spot + 1}, device_id_type=MESH)


def meet(devices, count):
    spot = lax.axis_index("red")
    neighbours = jnp.where(spot > 0, 1, 0) + jnp.where(spot < count - 1, 1, 0)
    pl.semaphore_wait(pltpu.get_barrier_semaphore(), devices - 1 + neighbours)


def exchange(devices, source, target, send_sem, recv_sem, base):
    me = lax.axis_index("seq")
    copies = []
    for step in range(1, devices):
        peer = lax.rem(me + step, devices)
        copy = pltpu.make_async_remote_copy(
            src_ref=source(peer),
            dst_ref=target(me),
            send_sem=send_sem.at[base + step - 1],
            recv_sem=recv_sem.at[base + step - 1],
            device_id={"seq": peer},
            device_id_type=MESH,
        )
        copy.start()
        copies.append(copy)
    return copies


def main_kernel(
    devices, count, chunks, scale_factor,
    tok_ref, emb_ref, wt_ref, filt_ref, cot_ref, high_hbm, low_hbm,
    recv_ref, all_ref,
    part, from_left, from_right, out_sig, sig, sending, one_hot, high_ref, low_ref,
    table_sem, sig_send, sig_recv, res_send, res_recv,
    right_send, right_recv, left_send, left_recv,
    up_send, up_recv, down_send, down_recv,
):
    me = lax.axis_index("seq")
    spot = lax.axis_index("red")
    branches, _, piece, _ = wt_ref.shape
    tok_count, width = filt_ref.shape
    vocabulary = emb_ref.shape[0]
    sub = piece // chunks
    greet(devices, count)
    tables = [
        pltpu.make_async_copy(high_hbm, high_ref, table_sem.at[0]),
        pltpu.make_async_copy(low_hbm, low_ref, table_sem.at[1]),
    ]
    for copy in tables:
        copy.start()
    above_spot = jnp.minimum(spot + 1, count - 1)
    below_spot = jnp.maximum(spot - 1, 0)

    def hop(source, target, slot, sends, recvs, neighbour):
        return pltpu.make_async_remote_copy(
            src_ref=source.at[slot],
            dst_ref=target.at[slot],
            send_sem=sends.at[slot],
            recv_sem=recvs.at[slot],
            device_id={"red": neighbour},
            device_id_type=MESH,
        )

    def place(chunk, branch):
        return (chunk * branches + branch) * count

    def right(slot):
        return hop(part, from_left, slot, right_send, right_recv, above_spot)

    def left(slot):
        return hop(part, from_right, slot, left_send, left_recv, below_spot)

    def up(slot):
        return hop(all_ref, all_ref, slot, up_send, up_recv, above_spot)

    def down(slot):
        return hop(all_ref, all_ref, slot, down_send, down_recv, below_spot)

    def products(chunk):
        table = emb_ref[...]
        for group in range(count):
            rows = [wt_ref[b, group, chunk * sub : (chunk + 1) * sub] for b in range(branches)]
            product = dot(jnp.concatenate(rows, axis=0), table, NT)
            for b in range(branches):
                part[place(chunk, b) + group] = product[b * sub : (b + 1) * sub]

    def first_hops(chunk):
        bases = [place(chunk, branch) for branch in range(branches)]

        @pl.when(spot == 0)
        def _():
            for goal in range(count - 1, 0, -1):
                for base in bases:
                    right(base + goal).start()

        @pl.when(spot == count - 1)
        def _():
            for goal in range(count - 1):
                for base in bases:
                    left(base + goal).start()

    def middle_hops(chunk):
        for tick in range(1, count - 1):
            for branch in range(branches):
                later_hop(place(chunk, branch), tick)

    def later_hop(base, tick):
        goal = count - 1 - (tick - spot)

        @pl.when((spot > 0) & (tick >= spot) & (spot < goal))
        def _():
            right(base + goal).wait_recv()
            part[base + goal] = part[base + goal] + from_left[base + goal]
            right(base + goal).start()

        other = tick - (count - 1 - spot)

        @pl.when((spot < count - 1) & (other >= 0) & (spot > other))
        def _():
            left(base + other).wait_recv()
            part[base + other] = part[base + other] + from_right[base + other]
            left(base + other).start()

    def arrive(chunk):
        for branch in range(branches):
            slot = place(chunk, branch) + spot

            @pl.when(spot > 0)
            def _():
                right(slot).wait_recv()
                part[slot] = part[slot] + from_left[slot]

            @pl.when(spot < count - 1)
            def _():
                left(slot).wait_recv()
                part[slot] = part[slot] + from_right[slot]

        slots = [place(chunk, branch) + spot for branch in range(branches)]
        return jnp.concatenate([part[slot] for slot in slots], axis=0)

    def share(chunk):
        for branch in range(branches):
            slot = place(chunk, branch) + spot

            @pl.when(spot < count - 1)
            def _():
                up(slot).start()

            @pl.when(spot > 0)
            def _():
                down(slot).start()

    def relay(chunk, step):
        for branch in range(branches):
            relay_block(place(chunk, branch), step)

    def relay_block(base, step):
        below = spot - step

        @pl.when(below >= 0)
        def _():
            up(base + below).wait_recv()

            @pl.when(spot < count - 1)
            def _():
                up(base + below).start()

        above = spot + step

        @pl.when(above < count)
        def _():
            down(base + above).wait_recv()

            @pl.when(spot > 0)
            def _():
                down(base + above).start()

    def signal_rows(start, rows):
        return jnp.concatenate([sig[at, start : start + rows] for at in range(devices)], axis=1)

    def channels(chunk, own, beside):
        projected = dot_split(own, one_hot[...])
        queries = projected[:sub]
        key_rows = projected[sub : 2 * sub]
        value_rows = projected[2 * sub :]
        filters = signal_rows(chunk * sub, sub)
        cotangent = signal_rows(piece + chunk * sub, sub)
        signals = jnp.concatenate([filters, key_rows * value_rows, cotangent * queries], axis=0)
        results = convolve(signals, high_ref, low_ref, sub, beside)
        rounded = []
        for at in range(devices):
            lanes = slice(at * tok_count, (at + 1) * tok_count)
            conv = results[at][:sub]
            grad_inner = results[at][sub : 2 * sub]
            grads = jnp.concatenate(
                [
                    cotangent[:, lanes] * conv,
                    grad_inner * value_rows[:, lanes],
                    grad_inner * key_rows[:, lanes],
                ],
                axis=0,
            ).astype(jnp.bfloat16)
            rounded.append(grads)
            sending[chunk, at, :sub] = queries[:, lanes] * conv
            sending[chunk, at, sub : 2 * sub] = results[at][2 * sub :] * scale_factor
            sending[chunk, at, 2 * sub :] = grads.astype(jnp.float32)
        sums = dot(jnp.concatenate(rounded, axis=1), one_hot[...], NT)
        for b in range(branches):
            all_ref[place(chunk, b) + spot] = sums[b * sub : (b + 1) * sub]

    filt_t = filt_ref[...].T
    cot_t = cot_ref[...].T
    tok_rows = jnp.broadcast_to(tok_ref[...].astype(jnp.float32), (8, tok_count))
    for peer in range(devices):
        out_sig[peer, :piece] = filt_t[peer * piece : (peer + 1) * piece]
        out_sig[peer, piece : 2 * piece] = cot_t[peer * piece : (peer + 1) * piece]
        out_sig[peer, 2 * piece :] = tok_rows
    products(0)
    meet(devices, count)
    first_hops(0)
    copies = exchange(devices, out_sig.at.__getitem__, sig.at.__getitem__, sig_send, sig_recv, 0)
    for chunk in range(1, chunks):
        products(chunk)
        first_hops(chunk)
    sig[me] = out_sig[me]
    for copy in copies:
        copy.wait_recv()
    ids = signal_rows(2 * piece, 1).astype(jnp.int32)
    vocab_rows = lax.broadcasted_iota(jnp.int32, (vocabulary, devices * tok_count), 0)
    one_hot[...] = jnp.where(vocab_rows == ids, 1.0, 0.0).astype(jnp.bfloat16)
    sent = list(copies)
    arrivals = []
    for chunk in range(chunks):
        middle_hops(chunk)
        if chunk > 0:
            relay(chunk - 1, 1)
        own = arrive(chunk)
        if chunk == 0:
            for copy in tables:
                copy.wait()

        def beside(chunk=chunk):
            if chunk > 0 and count > 2:
                relay(chunk - 1, 2)

        channels(chunk, own, beside)
        share(chunk)
        more = exchange(
            devices,
            lambda peer, chunk=chunk: sending.at[chunk, peer],
            lambda slot, chunk=chunk: recv_ref.at[chunk, slot],
            res_send, res_recv, chunk * (devices - 1),
        )
        recv_ref[chunk, me] = sending[chunk, me]
        sent += more
        arrivals += more
        if chunk > 0:
            for step in range(3, count):
                relay(chunk - 1, step)
    for step in range(1, count):
        relay(chunks - 1, step)
    for base in range(0, chunks * branches * count, count):
        for goal in range(count):
            @pl.when(spot < goal)
            def _():
                right(base + goal).wait_send()

            @pl.when(spot > goal)
            def _():
                left(base + goal).wait_send()

        for step in range(count):
            @pl.when((spot - step >= 0) & (spot < count - 1))
            def _():
                up(base + spot - step).wait_send()

            @pl.when((spot + step < count) & (spot > 0))
            def _():
                down(base + spot + step).wait_send()

    for copy in sent:
        copy.wait_send()
    for copy in arrivals:
        copy.wait_recv()


def final_kernel(scale_factor, emb_ref, recv_ref, all_ref, out_ref, filt_ref, grads_ref, weight_ref):
    chunks, devices, rows, _ = recv_ref.shape
    sub = rows // 5
    count = all_ref.shape[0] // (chunks * 3)
    table = emb_ref[...]
    for chunk in range(chunks):
        for group in range(count):
            blocks = [all_ref[(chunk * 3 + branch) * count + group] for branch in range(3)]
            product = dot_split(jnp.concatenate(blocks, axis=0), table) * scale_factor
            for branch in range(3):
                weight_ref[branch, group, chunk * sub : (chunk + 1) * sub] = product[
                    branch * sub : (branch + 1) * sub
                ]

    def positions(at):
        parts = [
            recv_ref[chunk, peer, at * sub : (at + 1) * sub]
            for peer in range(devices)
            for chunk in range(chunks)
        ]
        return jnp.concatenate(parts, axis=0).T

    out_ref[...] = positions(0)
    filt_ref[...] = positions(1)
    for branch in range(3):
        grads_ref[branch] = positions(2 + branch).astype(jnp.bfloat16)


def kernel_shards(devices, count, token_ids, embedding, proj_weight, filters, cotangent):
    tok_count, width = filters.shape
    vocabulary, depth = embedding.shape
    _, branches, _, piece = proj_weight.shape
    scale_factor = float(tok_count * devices) ** (-0.5)
    chunks = CHUNKS
    rows = piece // chunks
    f32 = jnp.float32
    dma = pltpu.SemaphoreType.DMA
    weight_t = jnp.transpose(proj_weight, (1, 2, 3, 0))
    high, low = transform_tables(tok_count, devices)
    block = (chunks * branches * count, rows, vocabulary)
    message = (devices, 2 * piece + 8, tok_count)
    answer = (chunks, devices, 5 * piece // chunks, tok_count)
    received, all_sums = pl.pallas_call(
        functools.partial(main_kernel, devices, count, chunks, scale_factor),
        out_shape=(jax.ShapeDtypeStruct(answer, f32), jax.ShapeDtypeStruct(block, f32)),
        in_specs=[VMEM] * 5 + [pl.BlockSpec(memory_space=pl.ANY)] * 2,
        out_specs=(VMEM, VMEM),
        scratch_shapes=[
            pltpu.VMEM(block, f32),
            pltpu.VMEM(block, f32),
            pltpu.VMEM(block, f32),
            pltpu.VMEM(message, f32),
            pltpu.VMEM(message, f32),
            pltpu.VMEM(answer, f32),
            pltpu.VMEM((vocabulary, devices * tok_count), jnp.bfloat16),
            pltpu.VMEM(high.shape, jnp.bfloat16),
            pltpu.VMEM(low.shape, jnp.bfloat16),
            dma((2,)),
            dma((devices - 1,)),
            dma((devices - 1,)),
            dma((chunks * (devices - 1),)),
            dma((chunks * (devices - 1),)),
        ]
        + [dma((chunks * branches * count,))] * 8,
        compiler_params=pltpu.CompilerParams(collective_id=0, has_side_effects=True),
        name="hyena_exchange",
    )(
        token_ids.reshape(1, tok_count), embedding, weight_t, filters, cotangent,
        jnp.asarray(high), jnp.asarray(low),
    )
    output, filter_grad, grads, weight = pl.pallas_call(
        functools.partial(final_kernel, scale_factor),
        out_shape=(
            jax.ShapeDtypeStruct((tok_count, width), f32),
            jax.ShapeDtypeStruct((tok_count, width), f32),
            jax.ShapeDtypeStruct((branches, tok_count, width), jnp.bfloat16),
            jax.ShapeDtypeStruct((branches, count, piece, depth), f32),
        ),
        in_specs=[VMEM] * 3,
        out_specs=(VMEM,) * 4,
        name="finish",
    )(embedding, received, all_sums)
    return (
        output,
        filter_grad,
        jnp.transpose(grads, (1, 0, 2)),
        jnp.transpose(weight, (3, 0, 1, 2)),
    )


def fits_kernels(devices, count, token_ids, embedding, proj_weight, filters):
    tok_count, width = filters.shape
    vocabulary, depth = embedding.shape
    _, branches, red_count, piece = proj_weight.shape
    lanes = (tok_count, vocabulary, depth)
    aligned = all(size % 128 == 0 for size in lanes) and piece % (16 * CHUNKS) == 0
    tables = devices * (2 * tok_count) ** 2 * 4
    one_hot = vocabulary * tok_count * devices * 8
    held = 4 * branches * piece * vocabulary * (3 * count + 2)
    return (
        aligned
        and branches == 3
        and red_count == count
        and width == devices * piece
        and tables + one_hot + held < 40 * 2**20
    )


def angles(numbers, modulus, direction):
    phase = (numbers % modulus).astype(jnp.float32) * (direction * 2.0 * math.pi / modulus)
    return (jnp.cos(phase), jnp.sin(phase))


def rotate(real_part, imag_part, cosine, sine_part):
    return (real_part * cosine - imag_part * sine_part, real_part * sine_part + imag_part * cosine)


def complex_einsum(formula, matrix, values):
    mat_real, mat_imag = matrix
    val_real, val_imag = values
    real_out = jnp.einsum(formula, mat_real, val_real, precision=precise_mode) - jnp.einsum(
        formula, mat_imag, val_imag, precision=precise_mode
    )
    imag_out = jnp.einsum(formula, mat_real, val_imag, precision=precise_mode) + jnp.einsum(
        formula, mat_imag, val_real, precision=precise_mode
    )
    return (real_out, imag_out)


def factors(length_total):
    first_factor = 1
    for candidate in range(1, math.isqrt(length_total) + 1):
        if length_total % candidate == 0:
            first_factor = candidate
    return (first_factor, length_total // first_factor)


def combine_spectra(spec_real, spec_imag, width):
    filt_re = spec_real[..., :width]
    inner_re = spec_real[..., width : 2 * width]
    up_re = spec_real[..., 2 * width :]
    filt_im = spec_imag[..., :width]
    inner_im = spec_imag[..., width : 2 * width]
    up_im = spec_imag[..., 2 * width :]
    joined_real = jnp.concatenate(
        [
            filt_re * inner_re - filt_im * inner_im,
            filt_re * up_re + filt_im * up_im,
            up_re * inner_re + up_im * inner_im,
        ],
        axis=-1,
    )
    joined_imag = jnp.concatenate(
        [
            filt_re * inner_im + filt_im * inner_re,
            filt_re * up_im - filt_im * up_re,
            up_im * inner_re - up_re * inner_im,
        ],
        axis=-1,
    )
    return (joined_real, joined_imag)


def local_convolve(signals):
    length, branch_count, narrow = signals.shape
    total = 2 * length
    first_factor, second_factor = factors(total)
    flat = signals.reshape(length, branch_count * narrow)
    padded = jnp.concatenate([flat, jnp.zeros_like(flat)], axis=0).reshape(
        first_factor, second_factor, branch_count * narrow
    )
    first_index = jnp.arange(first_factor, dtype=jnp.int32)
    second_index = jnp.arange(second_factor, dtype=jnp.int32)
    cosine, sine_part = angles(first_index[:, None] * first_index[None, :], first_factor, -1.0)
    real_part = jnp.einsum("kn,nbm->kbm", cosine, padded, precision=precise_mode)
    imag_part = jnp.einsum("kn,nbm->kbm", sine_part, padded, precision=precise_mode)
    cosine, sine_part = angles(first_index[:, None] * second_index[None, :], total, -1.0)
    real_part, imag_part = rotate(real_part, imag_part, cosine[:, :, None], sine_part[:, :, None])
    real_part, imag_part = complex_einsum(
        "lb,kbm->klm",
        angles(second_index[:, None] * second_index[None, :], second_factor, -1.0),
        (real_part, imag_part),
    )
    real_part, imag_part = combine_spectra(real_part, imag_part, narrow)
    real_part, imag_part = complex_einsum(
        "bl,klm->kbm",
        angles(second_index[:, None] * second_index[None, :], second_factor, 1.0),
        (real_part, imag_part),
    )
    cosine, sine_part = angles(first_index[:, None] * second_index[None, :], total, 1.0)
    real_part, imag_part = rotate(real_part, imag_part, cosine[:, :, None], sine_part[:, :, None])
    cosine, sine_part = angles(first_index[:, None] * first_index[None, :], first_factor, 1.0)
    result = jnp.einsum("nk,kbm->nbm", cosine, real_part, precision=precise_mode) - jnp.einsum(
        "nk,kbm->nbm", sine_part, imag_part, precision=precise_mode
    )
    result = result.reshape(total, branch_count * narrow)[:length] / total
    return result.reshape(length, branch_count, narrow)


def shards(token_ids, embedding, proj_weight, filters, cotangent):
    tok_count = token_ids.shape[0]
    devices = lax.axis_size("seq")
    count = lax.axis_size("red")
    if fits_kernels(devices, count, token_ids, embedding, proj_weight, filters):
        return kernel_shards(
            devices, count, token_ids, embedding, proj_weight, filters, cotangent
        )
    width = filters.shape[1]
    vocabulary = embedding.shape[0]
    width_rows, branches, red_count, piece = proj_weight.shape
    scale_factor = float(tok_count * devices) ** (-0.5)
    table = jnp.dot(
        embedding,
        proj_weight.reshape(width_rows, branches * red_count * piece),
        preferred_element_type=jnp.float32,
    )
    table = table.reshape(vocabulary, branches, red_count, piece)
    own_table = lax.psum_scatter(table, "red", scatter_dimension=2, tiled=True)
    full_table = lax.all_gather(own_table, "seq", axis=3, tiled=True)
    projected = jnp.take(full_table, token_ids, axis=0)
    projected = projected.reshape(tok_count, branches, width)
    queries = projected[:, 0]
    key_rows = projected[:, 1]
    value_rows = projected[:, 2]
    inner = key_rows * value_rows
    upstream = cotangent * queries
    stacked = jnp.stack([filters, inner, upstream], axis=1)
    whole_length = lax.all_to_all(stacked, "seq", split_axis=2, concat_axis=0, tiled=True)
    results = local_convolve(whole_length)
    returned = lax.all_to_all(results, "seq", split_axis=0, concat_axis=2, tiled=True)
    conv = returned[:, 0]
    grad_inner = returned[:, 1]
    filter_raw = returned[:, 2]
    output = queries * conv
    filter_grad = filter_raw * scale_factor
    branch_grads = jnp.stack(
        [cotangent * conv, grad_inner * value_rows, grad_inner * key_rows], axis=1
    ).astype(jnp.bfloat16)
    one_hot = (token_ids[:, None] == lax.iota(jnp.int32, vocabulary)[None, :]).astype(jnp.bfloat16)
    token_sums = lax.dot_general(
        one_hot,
        branch_grads.reshape(tok_count, branches * width),
        (((0,), (0,)), ((), ())),
        preferred_element_type=jnp.float32,
    )
    summed = lax.psum_scatter(
        token_sums.reshape(vocabulary, branches, width), "seq", scatter_dimension=2, tiled=True
    )
    gathered = lax.all_gather(summed[:, :, None, :], "red", axis=2, tiled=True)
    weight_grad = (
        lax.dot_general(
            embedding.astype(jnp.float32),
            gathered.reshape(vocabulary, branches * red_count * piece),
            (((0,), (0,)), ((), ())),
            precision=precise_mode,
        )
        * scale_factor
    )
    return (
        output,
        filter_grad,
        branch_grads,
        weight_grad.reshape(width_rows, branches, red_count, piece),
    )


def solution(mesh):
    in_specs = (
        P("seq"),
        P(None, "red"),
        P("red", None, None, "seq"),
        P("seq", "red"),
        P("seq", "red"),
    )
    out_specs = (
        P("seq", "red"),
        P("seq", "red"),
        P("seq", None, "red"),
        P("red", None, None, "seq"),
    )
    return jax.shard_map(shards, mesh=mesh, in_specs=in_specs, out_specs=out_specs, check_vma=False)
```

```python
import functools
import math

import jax
import jax.numpy as jnp
import numpy as np
from jax import lax
from jax.experimental import pallas as pl
from jax.experimental.pallas import tpu as pltpu
from jax.sharding import PartitionSpec as P

precise_mode = lax.Precision.HIGHEST
MESH = pl.DeviceIdType.MESH
VMEM = pl.BlockSpec(memory_space=pltpu.VMEM)
CHUNKS = 1
NN = (((1,), (0,)), ((), ()))
NT = (((1,), (1,)), ((), ()))


def split(value):
    high = value.astype(jnp.bfloat16)
    low = (value - high.astype(jnp.float32)).astype(jnp.bfloat16)
    return high, low


def dot(left, right, dims=NN):
    return lax.dot_general(left, right, dims, preferred_element_type=jnp.float32)


def dot_split(value, matrix, dims=NN):
    high, low = split(value)
    both = dot(jnp.concatenate([high, low], axis=0), matrix, dims)
    rows = value.shape[0]
    return both[:rows] + both[rows:]


def dot_both(value, matrix_high, matrix_low, dims=NN):
    high, _ = split(value)
    return dot_split(value, matrix_high, dims) + dot(high, matrix_low, dims)


def transform_tables(block, blocks):
    total = 2 * blocks * block
    place = np.arange(block)
    half = block // 2
    tables = np.zeros((blocks, 2 * block, 2 * block))
    even = 2 * np.pi * ((2 * blocks * place[:, None] * np.arange(half)[None, :]) % total) / total
    odd = 2 * np.pi * ((place[:, None] * (blocks + 2 * blocks * np.arange(half))[None, :]) % total) / total
    tables[0, :block, :half] = np.cos(even)
    tables[0, :block, block : block + half] = np.sin(even)
    tables[0, :block, block] = 1.0 - 2.0 * (place % 2)
    tables[0, block:, half:block] = np.cos(odd)
    tables[0, block:, block + half :] = np.sin(odd)
    for residue in range(1, blocks):
        freq = residue + 2 * blocks * np.arange(block)
        psi = 2 * np.pi * ((place[:, None] * freq[None, :]) % total) / total
        tables[residue, :block, :block] = np.cos(psi)
        tables[residue, :block, block:] = np.sin(psi)
        tables[residue, block:, :block] = -np.sin(psi)
        tables[residue, block:, block:] = np.cos(psi)
    tables = tables.astype(np.float32)
    high = tables.astype(jnp.bfloat16)
    low = (tables - high.astype(np.float32)).astype(jnp.bfloat16)
    return high, low


def phases(residue, blocks):
    if residue == 0:
        return [1.0] * blocks, [(-1.0) ** index for index in range(blocks)]
    turn = [math.pi * ((residue * index) % (2 * blocks)) / blocks for index in range(blocks)]
    return [math.cos(a) for a in turn], [math.sin(a) for a in turn]


def weighted(terms, weights):
    total = None
    for term, weight in zip(terms, weights):
        if abs(weight) < 1e-12:
            continue
        part = term if weight == 1.0 else term * weight
        total = part if total is None else total + part
    return total


def convolve(signals, high_ref, low_ref, piece, beside):
    blocks, double, _ = high_ref.shape
    block = double // 2
    pieces = [signals[:, index * block : (index + 1) * block] for index in range(blocks)]
    results = [None] * blocks
    scale = 1.0 / (blocks * block)
    for residue in range(blocks):
        if residue == blocks // 2:
            beside()
        cosines, sines = phases(residue, blocks)
        packed = jnp.concatenate([weighted(pieces, cosines), weighted(pieces, sines)], axis=1)
        spectrum = dot_both(packed, high_ref[residue], low_ref[residue])
        cos_part = spectrum[:, :block]
        sin_part = spectrum[:, block:]
        fc, ic, uc = (cos_part[at * piece : (at + 1) * piece] for at in range(3))
        fs, i_s, us = (sin_part[at * piece : (at + 1) * piece] for at in range(3))
        cc = [fc * ic, fc * uc, uc * ic]
        ss = [fs * i_s, fs * us, us * i_s]
        signs = [-1.0, 1.0, 1.0]
        new_cos = [c + sign * s for c, s, sign in zip(cc, ss, signs)]
        new_sin = [fc * i_s + fs * ic, fc * us - fs * uc, us * ic - uc * i_s]
        new_cos = jnp.concatenate(new_cos, axis=0)
        new_sin = jnp.concatenate(new_sin, axis=0)
        if residue == 0:
            first = lax.broadcasted_iota(jnp.int32, new_cos.shape, 1) == 0
            new_cos = jnp.where(first, 0.5 * jnp.concatenate(cc, axis=0), new_cos)
            new_sin = jnp.where(first, 0.5 * jnp.concatenate(ss, axis=0), new_sin)
        joined = jnp.concatenate([new_cos, new_sin], axis=1) * scale
        back = dot_both(joined, high_ref[residue], low_ref[residue], NT)
        first_half = back[:, :block]
        second_half = back[:, block:]
        for index in range(blocks):
            term = weighted([first_half, second_half], [cosines[index], sines[index]])
            results[index] = term if results[index] is None else results[index] + term
    return results


def greet(devices, count):
    me = lax.axis_index("seq")
    spot = lax.axis_index("red")
    barrier = pltpu.get_barrier_semaphore()
    for step in range(1, devices):
        peer = lax.rem(me + step, devices)
        pl.semaphore_signal(barrier, inc=1, device_id={"seq": peer}, device_id_type=MESH)

    @pl.when(spot > 0)
    def _():
        pl.semaphore_signal(barrier, inc=1, device_id={"red": spot - 1}, device_id_type=MESH)

    @pl.when(spot < count - 1)
    def _():
        pl.semaphore_signal(barrier, inc=1, device_id={"red": spot + 1}, device_id_type=MESH)


def meet(devices, count):
    spot = lax.axis_index("red")
    neighbours = jnp.where(spot > 0, 1, 0) + jnp.where(spot < count - 1, 1, 0)
    pl.semaphore_wait(pltpu.get_barrier_semaphore(), devices - 1 + neighbours)


def exchange(devices, source, target, send_sem, recv_sem, base):
    me = lax.axis_index("seq")
    copies = []
    for step in range(1, devices):
        peer = lax.rem(me + step, devices)
        copy = pltpu.make_async_remote_copy(
            src_ref=source(peer),
            dst_ref=target(me),
            send_sem=send_sem.at[base + step - 1],
            recv_sem=recv_sem.at[base + step - 1],
            device_id={"seq": peer},
            device_id_type=MESH,
        )
        copy.start()
        copies.append(copy)
    return copies


def main_kernel(
    devices, count, chunks, scale_factor,
    tok_ref, emb_ref, wt_ref, filt_ref, cot_ref, high_hbm, low_hbm,
    recv_ref, all_ref,
    part, from_left, from_right, out_sig, sig, sending, one_hot, high_ref, low_ref,
    table_sem, sig_send, sig_recv, res_send, res_recv,
    right_send, right_recv, left_send, left_recv,
    up_send, up_recv, down_send, down_recv,
):
    me = lax.axis_index("seq")
    spot = lax.axis_index("red")
    branches, _, piece, _ = wt_ref.shape
    tok_count, width = filt_ref.shape
    vocabulary = emb_ref.shape[0]
    sub = piece // chunks
    greet(devices, count)
    tables = [
        pltpu.make_async_copy(high_hbm, high_ref, table_sem.at[0]),
        pltpu.make_async_copy(low_hbm, low_ref, table_sem.at[1]),
    ]
    for copy in tables:
        copy.start()
    above_spot = jnp.minimum(spot + 1, count - 1)
    below_spot = jnp.maximum(spot - 1, 0)

    def hop(source, target, slot, sends, recvs, neighbour):
        return pltpu.make_async_remote_copy(
            src_ref=source.at[slot],
            dst_ref=target.at[slot],
            send_sem=sends.at[slot],
            recv_sem=recvs.at[slot],
            device_id={"red": neighbour},
            device_id_type=MESH,
        )

    def place(chunk, branch):
        return (chunk * branches + branch) * count

    def right(slot):
        return hop(part, from_left, slot, right_send, right_recv, above_spot)

    def left(slot):
        return hop(part, from_right, slot, left_send, left_recv, below_spot)

    def up(slot):
        return hop(all_ref, all_ref, slot, up_send, up_recv, above_spot)

    def down(slot):
        return hop(all_ref, all_ref, slot, down_send, down_recv, below_spot)

    def products(chunk):
        table = emb_ref[...]
        for group in range(count):
            rows = [wt_ref[b, group, chunk * sub : (chunk + 1) * sub] for b in range(branches)]
            product = dot(jnp.concatenate(rows, axis=0), table, NT)
            for b in range(branches):
                part[place(chunk, b) + group] = product[b * sub : (b + 1) * sub]

    def first_hops(chunk):
        bases = [place(chunk, branch) for branch in range(branches)]

        @pl.when(spot == 0)
        def _():
            for goal in range(count - 1, 0, -1):
                for base in bases:
                    right(base + goal).start()

        @pl.when(spot == count - 1)
        def _():
            for goal in range(count - 1):
                for base in bases:
                    left(base + goal).start()

    def middle_hops(chunk):
        for tick in range(1, count - 1):
            for branch in range(branches):
                later_hop(place(chunk, branch), tick)

    def later_hop(base, tick):
        goal = count - 1 - (tick - spot)

        @pl.when((spot > 0) & (tick >= spot) & (spot < goal))
        def _():
            right(base + goal).wait_recv()
            part[base + goal] = part[base + goal] + from_left[base + goal]
            right(base + goal).start()

        other = tick - (count - 1 - spot)

        @pl.when((spot < count - 1) & (other >= 0) & (spot > other))
        def _():
            left(base + other).wait_recv()
            part[base + other] = part[base + other] + from_right[base + other]
            left(base + other).start()

    def arrive(chunk):
        for branch in range(branches):
            slot = place(chunk, branch) + spot

            @pl.when(spot > 0)
            def _():
                right(slot).wait_recv()
                part[slot] = part[slot] + from_left[slot]

            @pl.when(spot < count - 1)
            def _():
                left(slot).wait_recv()
                part[slot] = part[slot] + from_right[slot]

        slots = [place(chunk, branch) + spot for branch in range(branches)]
        return jnp.concatenate([part[slot] for slot in slots], axis=0)

    def share(chunk):
        for branch in range(branches):
            slot = place(chunk, branch) + spot

            @pl.when(spot < count - 1)
            def _():
                up(slot).start()

            @pl.when(spot > 0)
            def _():
                down(slot).start()

    def relay(chunk, step):
        for branch in range(branches):
            relay_block(place(chunk, branch), step)

    def relay_block(base, step):
        below = spot - step

        @pl.when(below >= 0)
        def _():
            up(base + below).wait_recv()

            @pl.when(spot < count - 1)
            def _():
                up(base + below).start()

        above = spot + step

        @pl.when(above < count)
        def _():
            down(base + above).wait_recv()

            @pl.when(spot > 0)
            def _():
                down(base + above).start()

    def signal_rows(start, rows):
        return jnp.concatenate([sig[at, start : start + rows] for at in range(devices)], axis=1)

    def channels(chunk, own, beside):
        projected = dot_split(own, one_hot[...])
        queries = projected[:sub]
        key_rows = projected[sub : 2 * sub]
        value_rows = projected[2 * sub :]
        filters = signal_rows(chunk * sub, sub)
        cotangent = signal_rows(piece + chunk * sub, sub)
        signals = jnp.concatenate([filters, key_rows * value_rows, cotangent * queries], axis=0)
        results = convolve(signals, high_ref, low_ref, sub, beside)
        rounded = []
        for at in range(devices):
            lanes = slice(at * tok_count, (at + 1) * tok_count)
            conv = results[at][:sub]
            grad_inner = results[at][sub : 2 * sub]
            grads = jnp.concatenate(
                [
                    cotangent[:, lanes] * conv,
                    grad_inner * value_rows[:, lanes],
                    grad_inner * key_rows[:, lanes],
                ],
                axis=0,
            ).astype(jnp.bfloat16)
            rounded.append(grads)
            sending[chunk, at, :sub] = queries[:, lanes] * conv
            sending[chunk, at, sub : 2 * sub] = results[at][2 * sub :] * scale_factor
            sending[chunk, at, 2 * sub :] = grads.astype(jnp.float32)
        sums = dot(jnp.concatenate(rounded, axis=1), one_hot[...], NT)
        for b in range(branches):
            all_ref[place(chunk, b) + spot] = sums[b * sub : (b + 1) * sub]

    filt_t = filt_ref[...].T
    cot_t = cot_ref[...].T
    tok_rows = jnp.broadcast_to(tok_ref[...].astype(jnp.float32), (8, tok_count))
    for peer in range(devices):
        out_sig[peer, :piece] = filt_t[peer * piece : (peer + 1) * piece]
        out_sig[peer, piece : 2 * piece] = cot_t[peer * piece : (peer + 1) * piece]
        out_sig[peer, 2 * piece :] = tok_rows
    products(0)
    meet(devices, count)
    first_hops(0)
    copies = exchange(devices, out_sig.at.__getitem__, sig.at.__getitem__, sig_send, sig_recv, 0)
    for chunk in range(1, chunks):
        products(chunk)
        first_hops(chunk)
    sig[me] = out_sig[me]
    for copy in copies:
        copy.wait_recv()
    ids = signal_rows(2 * piece, 1).astype(jnp.int32)
    vocab_rows = lax.broadcasted_iota(jnp.int32, (vocabulary, devices * tok_count), 0)
    one_hot[...] = jnp.where(vocab_rows == ids, 1.0, 0.0).astype(jnp.bfloat16)
    sent = list(copies)
    arrivals = []
    for chunk in range(chunks):
        middle_hops(chunk)
        if chunk > 0:
            relay(chunk - 1, 1)
        own = arrive(chunk)
        if chunk == 0:
            for copy in tables:
                copy.wait()

        def beside(chunk=chunk):
            if chunk > 0 and count > 2:
                relay(chunk - 1, 2)

        channels(chunk, own, beside)
        share(chunk)
        more = exchange(
            devices,
            lambda peer, chunk=chunk: sending.at[chunk, peer],
            lambda slot, chunk=chunk: recv_ref.at[chunk, slot],
            res_send, res_recv, chunk * (devices - 1),
        )
        recv_ref[chunk, me] = sending[chunk, me]
        sent += more
        arrivals += more
        if chunk > 0:
            for step in range(3, count):
                relay(chunk - 1, step)
    for step in range(1, count):
        relay(chunks - 1, step)
    for base in range(0, chunks * branches * count, count):
        for goal in range(count):
            @pl.when(spot < goal)
            def _():
                right(base + goal).wait_send()

            @pl.when(spot > goal)
            def _():
                left(base + goal).wait_send()

        for step in range(count):
            @pl.when((spot - step >= 0) & (spot < count - 1))
            def _():
                up(base + spot - step).wait_send()

            @pl.when((spot + step < count) & (spot > 0))
            def _():
                down(base + spot + step).wait_send()

    for copy in sent:
        copy.wait_send()
    for copy in arrivals:
        copy.wait_recv()


def final_kernel(scale_factor, emb_ref, recv_ref, all_ref, out_ref, filt_ref, grads_ref, weight_ref):
    chunks, devices, rows, _ = recv_ref.shape
    sub = rows // 5
    table = emb_ref[...]
    for chunk in range(chunks):
        blocks = [all_ref[chunk * 3 + branch, 0] for branch in range(3)]
        product = dot_split(jnp.concatenate(blocks, axis=0), table) * scale_factor
        for branch in range(3):
            weight_ref[branch, 0, chunk * sub : (chunk + 1) * sub] = product[
                branch * sub : (branch + 1) * sub
            ]

    def positions(at):
        parts = [
            recv_ref[chunk, peer, at * sub : (at + 1) * sub]
            for peer in range(devices)
            for chunk in range(chunks)
        ]
        return jnp.concatenate(parts, axis=0).T

    @pl.when(pl.program_id(0) == 0)
    def _():
        out_ref[...] = positions(0)
        filt_ref[...] = positions(1)
        for branch in range(3):
            grads_ref[branch] = positions(2 + branch).astype(jnp.bfloat16)


def kernel_shards(devices, count, token_ids, embedding, proj_weight, filters, cotangent):
    tok_count, width = filters.shape
    vocabulary, depth = embedding.shape
    _, branches, _, piece = proj_weight.shape
    scale_factor = float(tok_count * devices) ** (-0.5)
    chunks = CHUNKS
    rows = piece // chunks
    f32 = jnp.float32
    dma = pltpu.SemaphoreType.DMA
    weight_t = jnp.transpose(proj_weight, (1, 2, 3, 0))
    high, low = transform_tables(tok_count, devices)
    block = (chunks * branches * count, rows, vocabulary)
    message = (devices, 2 * piece + 8, tok_count)
    answer = (chunks, devices, 5 * piece // chunks, tok_count)
    received, all_sums = pl.pallas_call(
        functools.partial(main_kernel, devices, count, chunks, scale_factor),
        out_shape=(jax.ShapeDtypeStruct(answer, f32), jax.ShapeDtypeStruct(block, f32)),
        in_specs=[VMEM] * 5 + [pl.BlockSpec(memory_space=pl.ANY)] * 2,
        out_specs=(VMEM, VMEM),
        scratch_shapes=[
            pltpu.VMEM(block, f32),
            pltpu.VMEM(block, f32),
            pltpu.VMEM(block, f32),
            pltpu.VMEM(message, f32),
            pltpu.VMEM(message, f32),
            pltpu.VMEM(answer, f32),
            pltpu.VMEM((vocabulary, devices * tok_count), jnp.bfloat16),
            pltpu.VMEM(high.shape, jnp.bfloat16),
            pltpu.VMEM(low.shape, jnp.bfloat16),
            dma((2,)),
            dma((devices - 1,)),
            dma((devices - 1,)),
            dma((chunks * (devices - 1),)),
            dma((chunks * (devices - 1),)),
        ]
        + [dma((chunks * branches * count,))] * 8,
        compiler_params=pltpu.CompilerParams(collective_id=0, has_side_effects=True),
        name="hyena_exchange",
    )(
        token_ids.reshape(1, tok_count), embedding, weight_t, filters, cotangent,
        jnp.asarray(high), jnp.asarray(low),
    )
    output, filter_grad, grads, weight = pl.pallas_call(
        functools.partial(final_kernel, scale_factor),
        out_shape=(
            jax.ShapeDtypeStruct((tok_count, width), f32),
            jax.ShapeDtypeStruct((tok_count, width), f32),
            jax.ShapeDtypeStruct((branches, tok_count, width), jnp.bfloat16),
            jax.ShapeDtypeStruct((branches, count, piece, depth), f32),
        ),
        grid=(count,),
        in_specs=[
            pl.BlockSpec(embedding.shape, lambda group: (0, 0)),
            pl.BlockSpec(answer, lambda group: (0, 0, 0, 0)),
            pl.BlockSpec((branches * chunks, 1, rows, vocabulary), lambda group: (0, group, 0, 0)),
        ],
        out_specs=(
            pl.BlockSpec((tok_count, width), lambda group: (0, 0)),
            pl.BlockSpec((tok_count, width), lambda group: (0, 0)),
            pl.BlockSpec((branches, tok_count, width), lambda group: (0, 0, 0)),
            pl.BlockSpec((branches, 1, piece, depth), lambda group: (0, group, 0, 0)),
        ),
        name="finish",
    )(embedding, received, all_sums.reshape(branches * chunks, count, rows, vocabulary))
    return (
        output,
        filter_grad,
        jnp.transpose(grads, (1, 0, 2)),
        jnp.transpose(weight, (3, 0, 1, 2)),
    )


def fits_kernels(devices, count, token_ids, embedding, proj_weight, filters):
    tok_count, width = filters.shape
    vocabulary, depth = embedding.shape
    _, branches, red_count, piece = proj_weight.shape
    lanes = (tok_count, vocabulary, depth)
    aligned = all(size % 128 == 0 for size in lanes) and piece % (16 * CHUNKS) == 0
    tables = devices * (2 * tok_count) ** 2 * 4
    one_hot = vocabulary * tok_count * devices * 8
    held = 4 * branches * piece * vocabulary * (3 * count + 2)
    return (
        aligned
        and branches == 3
        and red_count == count
        and width == devices * piece
        and tables + one_hot + held < 40 * 2**20
    )


def angles(numbers, modulus, direction):
    phase = (numbers % modulus).astype(jnp.float32) * (direction * 2.0 * math.pi / modulus)
    return (jnp.cos(phase), jnp.sin(phase))


def rotate(real_part, imag_part, cosine, sine_part):
    return (real_part * cosine - imag_part * sine_part, real_part * sine_part + imag_part * cosine)


def complex_einsum(formula, matrix, values):
    mat_real, mat_imag = matrix
    val_real, val_imag = values
    real_out = jnp.einsum(formula, mat_real, val_real, precision=precise_mode) - jnp.einsum(
        formula, mat_imag, val_imag, precision=precise_mode
    )
    imag_out = jnp.einsum(formula, mat_real, val_imag, precision=precise_mode) + jnp.einsum(
        formula, mat_imag, val_real, precision=precise_mode
    )
    return (real_out, imag_out)


def factors(length_total):
    first_factor = 1
    for candidate in range(1, math.isqrt(length_total) + 1):
        if length_total % candidate == 0:
            first_factor = candidate
    return (first_factor, length_total // first_factor)


def combine_spectra(spec_real, spec_imag, width):
    filt_re = spec_real[..., :width]
    inner_re = spec_real[..., width : 2 * width]
    up_re = spec_real[..., 2 * width :]
    filt_im = spec_imag[..., :width]
    inner_im = spec_imag[..., width : 2 * width]
    up_im = spec_imag[..., 2 * width :]
    joined_real = jnp.concatenate(
        [
            filt_re * inner_re - filt_im * inner_im,
            filt_re * up_re + filt_im * up_im,
            up_re * inner_re + up_im * inner_im,
        ],
        axis=-1,
    )
    joined_imag = jnp.concatenate(
        [
            filt_re * inner_im + filt_im * inner_re,
            filt_re * up_im - filt_im * up_re,
            up_im * inner_re - up_re * inner_im,
        ],
        axis=-1,
    )
    return (joined_real, joined_imag)


def local_convolve(signals):
    length, branch_count, narrow = signals.shape
    total = 2 * length
    first_factor, second_factor = factors(total)
    flat = signals.reshape(length, branch_count * narrow)
    padded = jnp.concatenate([flat, jnp.zeros_like(flat)], axis=0).reshape(
        first_factor, second_factor, branch_count * narrow
    )
    first_index = jnp.arange(first_factor, dtype=jnp.int32)
    second_index = jnp.arange(second_factor, dtype=jnp.int32)
    cosine, sine_part = angles(first_index[:, None] * first_index[None, :], first_factor, -1.0)
    real_part = jnp.einsum("kn,nbm->kbm", cosine, padded, precision=precise_mode)
    imag_part = jnp.einsum("kn,nbm->kbm", sine_part, padded, precision=precise_mode)
    cosine, sine_part = angles(first_index[:, None] * second_index[None, :], total, -1.0)
    real_part, imag_part = rotate(real_part, imag_part, cosine[:, :, None], sine_part[:, :, None])
    real_part, imag_part = complex_einsum(
        "lb,kbm->klm",
        angles(second_index[:, None] * second_index[None, :], second_factor, -1.0),
        (real_part, imag_part),
    )
    real_part, imag_part = combine_spectra(real_part, imag_part, narrow)
    real_part, imag_part = complex_einsum(
        "bl,klm->kbm",
        angles(second_index[:, None] * second_index[None, :], second_factor, 1.0),
        (real_part, imag_part),
    )
    cosine, sine_part = angles(first_index[:, None] * second_index[None, :], total, 1.0)
    real_part, imag_part = rotate(real_part, imag_part, cosine[:, :, None], sine_part[:, :, None])
    cosine, sine_part = angles(first_index[:, None] * first_index[None, :], first_factor, 1.0)
    result = jnp.einsum("nk,kbm->nbm", cosine, real_part, precision=precise_mode) - jnp.einsum(
        "nk,kbm->nbm", sine_part, imag_part, precision=precise_mode
    )
    result = result.reshape(total, branch_count * narrow)[:length] / total
    return result.reshape(length, branch_count, narrow)


def shards(token_ids, embedding, proj_weight, filters, cotangent):
    tok_count = token_ids.shape[0]
    devices = lax.axis_size("seq")
    count = lax.axis_size("red")
    if fits_kernels(devices, count, token_ids, embedding, proj_weight, filters):
        return kernel_shards(
            devices, count, token_ids, embedding, proj_weight, filters, cotangent
        )
    width = filters.shape[1]
    vocabulary = embedding.shape[0]
    width_rows, branches, red_count, piece = proj_weight.shape
    scale_factor = float(tok_count * devices) ** (-0.5)
    table = jnp.dot(
        embedding,
        proj_weight.reshape(width_rows, branches * red_count * piece),
        preferred_element_type=jnp.float32,
    )
    table = table.reshape(vocabulary, branches, red_count, piece)
    own_table = lax.psum_scatter(table, "red", scatter_dimension=2, tiled=True)
    full_table = lax.all_gather(own_table, "seq", axis=3, tiled=True)
    projected = jnp.take(full_table, token_ids, axis=0)
    projected = projected.reshape(tok_count, branches, width)
    queries = projected[:, 0]
    key_rows = projected[:, 1]
    value_rows = projected[:, 2]
    inner = key_rows * value_rows
    upstream = cotangent * queries
    stacked = jnp.stack([filters, inner, upstream], axis=1)
    whole_length = lax.all_to_all(stacked, "seq", split_axis=2, concat_axis=0, tiled=True)
    results = local_convolve(whole_length)
    returned = lax.all_to_all(results, "seq", split_axis=0, concat_axis=2, tiled=True)
    conv = returned[:, 0]
    grad_inner = returned[:, 1]
    filter_raw = returned[:, 2]
    output = queries * conv
    filter_grad = filter_raw * scale_factor
    branch_grads = jnp.stack(
        [cotangent * conv, grad_inner * value_rows, grad_inner * key_rows], axis=1
    ).astype(jnp.bfloat16)
    one_hot = (token_ids[:, None] == lax.iota(jnp.int32, vocabulary)[None, :]).astype(jnp.bfloat16)
    token_sums = lax.dot_general(
        one_hot,
        branch_grads.reshape(tok_count, branches * width),
        (((0,), (0,)), ((), ())),
        preferred_element_type=jnp.float32,
    )
    summed = lax.psum_scatter(
        token_sums.reshape(vocabulary, branches, width), "seq", scatter_dimension=2, tiled=True
    )
    gathered = lax.all_gather(summed[:, :, None, :], "red", axis=2, tiled=True)
    weight_grad = (
        lax.dot_general(
            embedding.astype(jnp.float32),
            gathered.reshape(vocabulary, branches * red_count * piece),
            (((0,), (0,)), ((), ())),
            precision=precise_mode,
        )
        * scale_factor
    )
    return (
        output,
        filter_grad,
        branch_grads,
        weight_grad.reshape(width_rows, branches, red_count, piece),
    )


def solution(mesh):
    in_specs = (
        P("seq"),
        P(None, "red"),
        P("red", None, None, "seq"),
        P("seq", "red"),
        P("seq", "red"),
    )
    out_specs = (
        P("seq", "red"),
        P("seq", "red"),
        P("seq", None, "red"),
        P("red", None, None, "seq"),
    )
    return jax.shard_map(shards, mesh=mesh, in_specs=in_specs, out_specs=out_specs, check_vma=False)
```
